128 devices in a mesh: row: 8 (over y, core), col: 16 (over z, x).
Axes of the slice: x: 4, y: 4, z: 4, core: 2. Of those that a mesh axis runs over, the one named last changes fastest.
Arguments:
- sens_blocks: float32 [1536, 16, 128, 128], P('row', 'col'), may hold values from -0.1875 to 0.1875
- block_rows: int32 [1536, 16], P('row', 'col'), may hold values from 0 to 127
- block_cols: int32 [1536, 16], P('row', 'col'), may hold values from 0 to 127
- block_count: int32 [8, 16], P('row', 'col'), may hold values from 24 to 192, as said below
- band_mask: int32 [262144], P('col'), may hold values 0 or 1
- level_set: float32 [262144], P('col'), may hold values from -6 to 6
- observed: float32 [131072], P('row'), may hold values from -6 to 6
- data_weight: float32 [131072], P('row'), may hold values from 0.5 to 2
Outputs:
- level_out: float32 [262144], P('col')
- misfit: float32 [131072], P('row')
The draws below stay inside these ranges and needn't reach their ends.
Inputs may be any that keep to these rules, and one draw needn't show every extreme that they name: `block_count`: on some device the count is exactly 192; the others hold between 24 and 96 live slots, drawn per device.
All inputs are finite; a program needn't handle non-finite values. No bound on the sum of `band_mask` on one device may be relied on, other than what follows from the above.
Results may differ from the reference program's by a relative error of at most 0.00015.
Values sent between devices are 32-bit elements; how exact they have to be, the bound alone decides.
No kernel may reach another device: no remote copies, remote signals or barrier semaphores. Data moves between devices by JAX's collectives and lax.ppermute only.
A program may use at most 128 MiB of HBM per device.

```python
import math
import jax
import jax.numpy as jnp
from jax import lax

BS = 128
RB_DEV = 128
CB_DEV = 128
NBLK = 192
GN_ITERS = 2
CG_ITERS = 4
NDATA = 131072
NCELL = 262144
N_ROW = 8
N_COL = 16


def draw_block_count(key, part):
    key_base = jax.random.fold_in(key, 11)
    key_top = jax.random.fold_in(key, 12)
    base = jax.random.randint(key_base, (N_ROW * N_COL,), NBLK // 8, NBLK // 2 + 1)
    top = jax.random.randint(key_top, (), 0, N_ROW * N_COL)
    flat = jnp.where(jnp.arange(N_ROW * N_COL) == top, NBLK, base)
    return flat.reshape(N_ROW, N_COL).astype(jnp.int32)


def place_ends(drawn, key, low, largest):
    longest = drawn.shape.index(max(drawn.shape))
    spots = []
    for shift in (0, 1):
        where = [jax.random.randint(jax.random.fold_in(key, axis), (), 0, length) for axis, length in enumerate(drawn.shape)]
        where[longest] = (where[longest] + shift) % drawn.shape[longest]
        spots.append(tuple(where))
    return drawn.at[spots[0]].set(low).at[spots[1]].set(largest)


def block_levels(own_key, shape, shards, least, high):
    gain, own = 1.0, jax.random.fold_in(own_key, 6)
    for axis_at, blocks in shards:
        heights = jnp.exp(jax.random.uniform(jax.random.fold_in(own, axis_at), (blocks,), jnp.float32, least / len(shards), high / len(shards)))
        gain = gain * jnp.repeat(heights, shape[axis_at] // blocks).reshape([-1 if axis == axis_at else 1 for axis in range(len(shape))])
    return gain


def normal_values(rng, extent, width, limit, shards=(), kind=jnp.bfloat16):
    loudness = block_levels(rng, extent, shards, -0.22, 0.18) if shards else 1.0
    result = jax.random.normal(rng, extent, jnp.float32) * width * loudness
    return jnp.minimum(jnp.maximum(result, -limit), limit).astype(kind)


def setup_inputs(seed: int = 0) -> dict:
    keys = jax.random.split(jax.random.key(seed), 9)
    return {
        "sens_blocks": normal_values(keys[0], (N_ROW * NBLK, N_COL, BS, BS), (BS * 8) ** -0.5, 0.1875, ((0, 8), (1, 16)), jnp.float32),
        "block_rows": place_ends(jax.random.randint(keys[1], (N_ROW * NBLK, N_COL), 0, RB_DEV), jax.random.fold_in(keys[1], 1), 0, RB_DEV - 1).astype(jnp.int32),
        "block_cols": place_ends(jax.random.randint(keys[2], (N_ROW * NBLK, N_COL), 0, CB_DEV), jax.random.fold_in(keys[2], 1), 0, CB_DEV - 1).astype(jnp.int32),
        "block_count": draw_block_count(jax.random.fold_in(keys[8], 71), 0),
        "band_mask": place_ends((jax.random.randint(keys[4], (NCELL,), 0, 2) < 1).astype(jnp.int32), jax.random.fold_in(keys[4], 1), 0, 1),
        "level_set": normal_values(keys[5], (NCELL,), 1.0, 6.0, ((0, 16),), jnp.float32),
        "observed": normal_values(keys[6], (NDATA,), 1.0, 6.0, ((0, 8),), jnp.float32),
        "data_weight": jnp.clip(jnp.exp(math.log(2.0) - 1.3862944 * jax.random.uniform(keys[7], (NDATA,), jnp.float32) ** block_levels(keys[7], (NDATA,), ((0, 8),), -0.2, 0.2)), 0.5, 2.0),
    }


def forward_all(blocks, rows, cols, live, cells):
    vb = cells.reshape(N_COL, CB_DEV, BS)
    cidx = jnp.arange(N_COL, dtype=jnp.int32)[None, None, :]
    picked = vb[cidx, cols]
    prod = jnp.einsum('rkcij,rkcj->rkci', blocks, picked, precision=lax.Precision.HIGHEST) * live[..., None]
    target = jnp.arange(N_ROW, dtype=jnp.int32)[:, None, None] * RB_DEV + rows
    out = jax.ops.segment_sum(prod.reshape(-1, BS), target.reshape(-1), num_segments=N_ROW * RB_DEV)
    return out.reshape(-1)


def adjoint_all(blocks, rows, cols, live, data):
    ub = data.reshape(N_ROW, RB_DEV, BS)
    ridx = jnp.arange(N_ROW, dtype=jnp.int32)[:, None, None]
    picked = ub[ridx, rows]
    prod = jnp.einsum('rkcij,rkci->rkcj', blocks, picked, precision=lax.Precision.HIGHEST) * live[..., None]
    target = jnp.arange(N_COL, dtype=jnp.int32)[None, None, :] * CB_DEV + cols
    out = jax.ops.segment_sum(prod.reshape(-1, BS), target.reshape(-1), num_segments=N_COL * CB_DEV)
    return out.reshape(-1)


def reference(sens_blocks, block_rows, block_cols, block_count, band_mask, level_set, observed, data_weight):
    blocks = sens_blocks.reshape(N_ROW, NBLK, N_COL, BS, BS)
    rows = block_rows.reshape(N_ROW, NBLK, N_COL)
    cols = block_cols.reshape(N_ROW, NBLK, N_COL)
    live = (jnp.arange(NBLK, dtype=jnp.int32)[None, :, None] < block_count[:, None, :]).astype(jnp.float32)
    band = band_mask.astype(jnp.float32)
    weight2 = data_weight * data_weight
    phi = level_set
    for outer in range(GN_ITERS):
        heavy = jax.nn.sigmoid(phi / 0.5)
        scale = band * heavy * (1.0 - heavy) / 0.5
        weighted = weight2 * (observed - forward_all(blocks, rows, cols, live, heavy))
        rhs = scale * adjoint_all(blocks, rows, cols, live, weighted)
        step = jnp.zeros_like(rhs)
        resid = rhs
        direction = rhs
        norm_now = jnp.sum(resid * resid)
        for inner in range(CG_ITERS):
            pushed = weight2 * forward_all(blocks, rows, cols, live, scale * direction)
            image = scale * adjoint_all(blocks, rows, cols, live, pushed) + 0.05 * band * direction
            alpha = norm_now / jnp.sum(direction * image)
            step = step + alpha * direction
            resid = resid - alpha * image
            if inner + 1 < CG_ITERS:
                norm_next = jnp.sum(resid * resid)
                direction = resid + (norm_next / norm_now) * direction
                norm_now = norm_next
        phi = phi + step
    misfit = data_weight * (observed - forward_all(blocks, rows, cols, live, jax.nn.sigmoid(phi / 0.5)))
    return phi, misfit
```

```python
import jax
import jax.numpy as jnp
from jax import lax
from jax.experimental import pallas as pl
from jax.experimental.pallas import tpu as pltpu
from jax.sharding import PartitionSpec as P

BS = 128
GN_ITERS = 2
CG_ITERS = 4
SLOTS = 192
GROUP = 16
ROWS = 136
TRASH = 135
F32, BF16 = jnp.float32, jnp.bfloat16

VMEM = pl.BlockSpec(memory_space=pltpu.VMEM)
SMEM = pl.BlockSpec(memory_space=pltpu.SMEM)
PARAMS = pltpu.CompilerParams(vmem_limit_bytes=16 << 20)
TILES = [pltpu.VMEM((128, 16, 128), BF16), pltpu.VMEM((128, 16, 128), BF16)]


def groups(count):
    return (count[0] + GROUP - 1) // GROUP


def split_kernel(count, sens, parts, buf, sem):
    total = groups(count)

    def copy(g, slot):
        return pltpu.make_async_copy(sens.at[pl.ds(g * GROUP, GROUP)], buf.at[slot], sem.at[slot])

    copy(0, 0).start()

    def body(g, carry):
        slot = lax.rem(g, 2)

        @pl.when(g + 1 < total)
        def _():
            copy(g + 1, 1 - slot).start()

        copy(g, slot).wait()
        for b in range(GROUP):
            value = buf[slot, b]
            high = value.astype(BF16)
            parts[g * GROUP + b, :, :BS] = high
            parts[g * GROUP + b, :, BS:] = (value - high.astype(F32)).astype(BF16)
        return carry

    lax.fori_loop(0, total, body, 0)


def split_blocks(count, sens):
    return pl.pallas_call(
        split_kernel,
        out_shape=pltpu.VMEM((SLOTS, BS, 2 * BS), BF16),
        in_specs=[SMEM, pl.BlockSpec(memory_space=pltpu.HBM)],
        out_specs=VMEM,
        scratch_shapes=[pltpu.VMEM((2, GROUP, BS, BS), F32), pltpu.SemaphoreType.DMA((2,))],
        compiler_params=PARAMS,
        name="split_blocks",
    )(count, pltpu.with_memory_space_constraint(sens, pltpu.HBM))


def fill_tiles(x, first, second):
    high = x.astype(BF16).astype(F32)
    low = x - high
    at = lax.broadcasted_iota(jnp.int32, (128, 16, BS), 1)
    high, low = high[:, None, :], low[:, None, :]
    first[...] = jnp.where(at == 0, high, jnp.where(at == 1, low, 0.0)).astype(BF16)
    second[...] = jnp.where(at == 2, high, jnp.where(at == 3, low, 0.0)).astype(BF16)


def forward_product(count, rows, cols, parts, x, out, first, second):
    fill_tiles(x, first, second)
    out[...] = jnp.zeros_like(out)

    def body(g, carry):
        for p in range(0, GROUP, 2):
            k = g * GROUP + p
            tile = first[cols[k]] + second[cols[k + 1]]
            r = lax.dot_general(
                jnp.concatenate([tile, tile], axis=1),
                parts[pl.ds(k, 2)].reshape(2 * BS, 2 * BS),
                (((1,), (1,)), ((), ())),
                preferred_element_type=F32,
            )
            out[pl.ds(rows[k], 1), :] += r[0:1, :BS] + r[1:2, :BS]
            out[pl.ds(rows[k + 1], 1), :] += r[2:3, BS:] + r[3:4, BS:]
        return carry

    lax.fori_loop(0, groups(count), body, 0)


def adjoint_product(count, rows, cols, parts, x, out, first, second):
    fill_tiles(x, first, second)
    out[...] = jnp.zeros_like(out)

    def body(g, carry):
        for p in range(0, GROUP, 2):
            k = g * GROUP + p
            r = lax.dot_general(
                jnp.concatenate([first[rows[k]], second[rows[k + 1]]], axis=1),
                parts[pl.ds(k, 2)].reshape(2 * BS, 2 * BS),
                (((1,), (0,)), ((), ())),
                preferred_element_type=F32,
            )
            r = r[0:8, :BS] + r[0:8, BS:]
            out[pl.ds(cols[k], 1), :] += r[0:1] + r[1:2]
            out[pl.ds(cols[k + 1], 1), :] += r[2:3] + r[3:4]
        return carry

    lax.fori_loop(0, groups(count), body, 0)


def aux_rows(out, *vectors):
    out[128:ROWS, :] = jnp.zeros((8, BS), F32)
    for i, v in enumerate(vectors):
        out[128 + i : 129 + i, :] = v


def column_sum(x):
    return jnp.sum(x, axis=0, keepdims=True)


def total(row):
    return jnp.sum(row, axis=1, keepdims=True)


def newton_direction(ga, gb, resid, direction, scal):
    d = resid + scal[2:3, :] * direction
    alpha = scal[0:1, :] / (total(ga + gb) + 0.05 * scal[1:2, :])
    return d, alpha


def start_kernel(with_update, count, rows, cols, parts, *refs):
    if with_update:
        phi, sa, sb, resid, direction, step, scal, band, out, scale, phi_out, first, second = refs
        d, alpha = newton_direction(sa[0:1, :], sb[0:1, :], resid[...], direction[...], scal[...])
        level = phi[...] + (step[...] + alpha * d)
        phi_out[...] = level
    else:
        phi, band, out, scale, first, second = refs
        level = phi[...]
    heavy = jax.nn.sigmoid(level / 0.5)
    scale[...] = band[...] * heavy * (1.0 - heavy) / 0.5
    forward_product(count, rows, cols, parts, heavy, out, first, second)
    aux_rows(out)


def misfit_kernel(count, rows, cols, parts, q0, q1, q2, q3, observed, weight, out, first, second):
    q = q0[:128, :] + q1[:128, :] + q2[:128, :] + q3[:128, :]
    w = weight[...]
    adjoint_product(count, rows, cols, parts, w * w * (observed[...] - q), out, first, second)
    aux_rows(out)


def rhs_kernel(count, rows, cols, parts, ga, gb, scale, out, resid, first, second):
    rhs = scale[...] * (ga[:128, :] + gb[:128, :])
    resid[...] = rhs
    forward_product(count, rows, cols, parts, scale[...] * rhs, out, first, second)
    aux_rows(out, column_sum(rhs * rhs))


def push_values(q0, q1, q2, q3, weight, pushed, scal):
    t = q0[:128, :] + q1[:128, :] + q2[:128, :] + q3[:128, :]
    sums = q0[128:ROWS, :] + q1[128:ROWS, :] + q2[128:ROWS, :] + q3[128:ROWS, :]
    rr = total(sums[0:1, :]) + jnp.zeros((1, BS), F32)
    if pushed is None:
        beta, dd, q = jnp.zeros((1, BS), F32), rr, t
    else:
        rd = total(sums[1:2, :])
        beta = rr / scal[0:1, :]
        dd = rr + 2.0 * beta * rd + beta * beta * scal[1:2, :]
        q = t + beta * pushed[...]
    w = weight[...]
    u = w * w * q
    return rr, dd, beta, q, u


def store_scalars(scal_out, rr, dd, beta):
    scal_out[...] = jnp.zeros((8, BS), F32)
    scal_out[0:1, :] = rr
    scal_out[1:2, :] = dd
    scal_out[2:3, :] = beta


def push_kernel(first_turn, count, rows, cols, parts, q0, q1, q2, q3, weight, *refs):
    if first_turn:
        pushed = scal = None
    else:
        pushed, scal, *refs = refs
    out, q_out, scal_out, first, second = refs
    rr, dd, beta, q, u = push_values(q0, q1, q2, q3, weight, pushed, scal)
    q_out[...] = q
    store_scalars(scal_out, rr, dd, beta)
    adjoint_product(count, rows, cols, parts, u, out, first, second)
    aux_rows(out, column_sum(u * q))


def last_push_kernel(q0, q1, q2, q3, weight, pushed, scal, out, scal_out):
    rr, dd, beta, q, u = push_values(q0, q1, q2, q3, weight, pushed, scal)
    store_scalars(scal_out, rr, dd, beta)
    out[...] = jnp.zeros((8, BS), F32)
    out[0:1, :] = column_sum(u * q)


def turn_kernel(first_turn, count, rows, cols, parts, ga, gb, scale, band, scal, resid, *refs):
    if first_turn:
        out, resid_out, direction_out, step_out, first, second = refs
        direction, step = jnp.zeros((128, BS), F32), jnp.zeros((128, BS), F32)
    else:
        direction, step, out, resid_out, direction_out, step_out, first, second = refs
        direction, step = direction[...], step[...]
    d, alpha = newton_direction(ga[128:129, :], gb[128:129, :], resid[...], direction, scal[...])
    image = scale[...] * (ga[:128, :] + gb[:128, :]) + 0.05 * band[...] * d
    r = resid[...] - alpha * image
    direction_out[...] = d
    step_out[...] = step + alpha * d
    resid_out[...] = r
    forward_product(count, rows, cols, parts, scale[...] * r, out, first, second)
    aux_rows(out, column_sum(r * r), column_sum(r * d))


def per_device(
    sens_blocks, block_rows, block_cols, block_count, band_mask, level_set, observed, data_weight
):
    count = block_count.reshape(1)
    row_ids, col_ids = block_rows.reshape(-1), block_cols.reshape(-1)
    live = jnp.arange(SLOTS, dtype=jnp.int32) < count[0]
    row_to, col_to = jnp.where(live, row_ids, TRASH), jnp.where(live, col_ids, TRASH)
    band = band_mask.astype(F32).reshape(128, BS)
    phi = level_set.reshape(128, BS)
    obs, weight = observed.reshape(128, BS), data_weight.reshape(128, BS)
    parts = split_blocks(count, sens_blocks.reshape(SLOTS, BS, BS))
    wide, plain, small = (pltpu.VMEM((n, BS), F32) for n in (ROWS, 128, 8))

    def product(kernel, forward, operands, outs, name):
        ids = (row_to, col_ids) if forward else (row_ids, col_to)
        return pl.pallas_call(
            kernel,
            out_shape=outs,
            in_specs=[SMEM] * 3 + [VMEM] * (1 + len(operands)),
            out_specs=[VMEM] * len(outs),
            scratch_shapes=TILES,
            compiler_params=PARAMS,
            name=name,
        )(count, *ids, parts, *operands)

    def exchange(value, axis, inner, along_outer):
        outer = 4
        shifts = range(1, outer if along_outer else inner)
        got = [value]
        for s in shifts:
            if along_outer:
                pairs = [(a * inner + b, (a + s) % outer * inner + b) for a in range(outer) for b in range(inner)]
            else:
                pairs = [(a * inner + b, a * inner + (b + s) % inner) for a in range(outer) for b in range(inner)]
            got.append(lax.ppermute(value, axis, pairs))
        return got

    def over_col(value):
        z = exchange(value, "col", 4, True)
        return exchange(z[0] + z[1] + z[2] + z[3], "col", 4, False)

    def over_row(value):
        y = exchange(value, "row", 2, True)
        return exchange(y[0] + y[1] + y[2] + y[3], "row", 2, False)

    def start(update):
        if update is None:
            out, scale = product(
                lambda *r: start_kernel(False, *r), True, (phi, band), [wide, plain], "start"
            )
            return out, scale, phi
        return product(
            lambda *r: start_kernel(True, *r), True, (*update, band), [wide, plain, plain], "restart"
        )

    update = None
    for outer in range(GN_ITERS):
        out, scale, phi = start(update)
        (out,) = product(misfit_kernel, False, (*over_col(out), obs, weight), [wide], "misfit")
        out, resid = product(rhs_kernel, True, (*over_row(out), scale), [wide, plain], "rhs")
        state, pushed = (), ()
        for turn in range(CG_ITERS - 1):
            out, q, scal = product(
                lambda *r, one=turn == 0: push_kernel(one, *r),
                False,
                (*over_col(out), weight, *pushed),
                [wide, plain, small],
                "push",
            )
            pushed = (q, scal)
            out, resid, direction, step = product(
                lambda *r, one=turn == 0: turn_kernel(one, *r),
                True,
                (*over_row(out), scale, band, scal, resid, *state),
                [wide, plain, plain, plain],
                "turn",
            )
            state = (direction, step)
        sums, scal = pl.pallas_call(
            last_push_kernel,
            out_shape=[small, small],
            in_specs=[VMEM] * 7,
            out_specs=[VMEM] * 2,
            compiler_params=PARAMS,
            name="last_push",
        )(*over_col(out), weight, *pushed)
        update = (phi, *over_row(sums), resid, direction, step, scal)
    out, _, phi = start(update)
    q = over_col(out)
    misfit = weight * (obs - (q[0] + q[1] + q[2] + q[3])[:128])
    return phi.reshape(-1), misfit.reshape(-1)


def solution(mesh):
    return jax.shard_map(
        per_device,
        mesh=mesh,
        in_specs=(
            P("row", "col", None, None),
            P("row", "col"),
            P("row", "col"),
            P("row", "col"),
            P("col"),
            P("col"),
            P("row"),
            P("row"),
        ),
        out_specs=(P("col"), P("row")),
        check_vma=False,
    )
```

```python
import jax
import jax.numpy as jnp
from jax import lax
from jax.experimental import pallas as pl
from jax.experimental.pallas import tpu as pltpu
from jax.sharding import PartitionSpec as P

BS = 128
GN_ITERS = 2
CG_ITERS = 4
SLOTS = 192
GROUP = 32
CHUNK = 16
ROWS_TO, COLS, ROWS_AT, COLS_TO, COUNT = 0, 192, 384, 576, 768
ROWS = 136
TRASH = 135
F32, BF16 = jnp.float32, jnp.bfloat16

VMEM = pl.BlockSpec(memory_space=pltpu.VMEM)
SMEM = pl.BlockSpec(memory_space=pltpu.SMEM)
PARAMS = pltpu.CompilerParams(vmem_limit_bytes=16 << 20)
TILES = [pltpu.VMEM((128, 16, 128), BF16), pltpu.VMEM((128, 16, 128), BF16)]


def groups(ids):
    return (ids[COUNT] + GROUP - 1) // GROUP


def split_kernel(ids, sens, parts, flipped, buf, sem):
    chunks = groups(ids) * (GROUP // CHUNK)

    def copy(g):
        at = pl.ds(g * CHUNK, CHUNK)
        return pltpu.make_async_copy(sens.at[at], buf.at[at], sem.at[g])

    def begin(g, carry):
        copy(g).start()
        return carry

    def body(g, carry):
        copy(g).wait()
        for b in range(CHUNK):
            k = g * CHUNK + b
            value = buf[k]
            for to, v in ((parts, value), (flipped, value.T)):
                high = v.astype(BF16)
                to[k, :, :BS] = high
                to[k, :, BS:] = (v - high.astype(F32)).astype(BF16)
        return carry

    lax.fori_loop(0, chunks, begin, 0)
    lax.fori_loop(0, chunks, body, 0)


def split_blocks(ids, sens):
    halves = pltpu.VMEM((SLOTS, BS, 2 * BS), BF16)
    return pl.pallas_call(
        split_kernel,
        out_shape=[halves, halves],
        in_specs=[SMEM, pl.BlockSpec(memory_space=pltpu.HBM)],
        out_specs=[VMEM, VMEM],
        scratch_shapes=[
            pltpu.VMEM((SLOTS, BS, BS), F32),
            pltpu.SemaphoreType.DMA((SLOTS // CHUNK,)),
        ],
        compiler_params=PARAMS,
        name="split_blocks",
    )(ids, pltpu.with_memory_space_constraint(sens, pltpu.HBM))


def fill_tiles(x, first, second):
    high = x.astype(BF16).astype(F32)
    low = x - high
    at = lax.broadcasted_iota(jnp.int32, (128, 16, BS), 1)
    high, low = high[:, None, :], low[:, None, :]
    first[...] = jnp.where(at == 0, high, jnp.where(at == 1, low, 0.0)).astype(BF16)
    second[...] = jnp.where(at == 2, high, jnp.where(at == 3, low, 0.0)).astype(BF16)


def product_of(source, target, ids, parts, x, out, first, second):
    fill_tiles(x, first, second)
    out[...] = jnp.zeros_like(out)

    def body(g, carry):
        for p in range(0, GROUP, 2):
            k = g * GROUP + p
            r = lax.dot_general(
                jnp.concatenate([first[ids[source + k]], second[ids[source + k + 1]]], axis=1),
                parts[pl.ds(k, 2)].reshape(2 * BS, 2 * BS),
                (((1,), (0,)), ((), ())),
                preferred_element_type=F32,
            )
            r = r[0:8, :BS] + r[0:8, BS:]
            out[pl.ds(ids[target + k], 1), :] += r[0:1] + r[1:2]
            out[pl.ds(ids[target + k + 1], 1), :] += r[2:3] + r[3:4]
        return carry

    lax.fori_loop(0, groups(ids), body, 0)


def forward_product(ids, flipped, x, out, first, second):
    product_of(COLS, ROWS_TO, ids, flipped, x, out, first, second)


def adjoint_product(ids, parts, x, out, first, second):
    product_of(ROWS_AT, COLS_TO, ids, parts, x, out, first, second)


def aux_rows(out, *vectors):
    out[128:ROWS, :] = jnp.zeros((8, BS), F32)
    for i, v in enumerate(vectors):
        out[128 + i : 129 + i, :] = v


def column_sum(x):
    return jnp.sum(x, axis=0, keepdims=True)


def total(row):
    return jnp.sum(row, axis=1, keepdims=True)


def newton_direction(ga, gb, resid, direction, scal):
    d = resid + scal[2:3, :] * direction
    alpha = scal[0:1, :] / (total(ga + gb) + 0.05 * scal[1:2, :])
    return d, alpha


def start_kernel(with_update, ids, parts, *refs):
    if with_update:
        phi, sa, sb, resid, direction, step, scal, band, out, scale, phi_out, first, second = refs
        d, alpha = newton_direction(sa[0:1, :], sb[0:1, :], resid[...], direction[...], scal[...])
        level = phi[...] + (step[...] + alpha * d)
        phi_out[...] = level
    else:
        phi, band, out, scale, first, second = refs
        level = phi[...]
    heavy = jax.nn.sigmoid(level / 0.5)
    scale[...] = band[...] * heavy * (1.0 - heavy) / 0.5
    forward_product(ids, parts, heavy, out, first, second)
    aux_rows(out)


def misfit_kernel(ids, parts, q0, q1, q2, q3, observed, weight, out, first, second):
    q = q0[:128, :] + q1[:128, :] + q2[:128, :] + q3[:128, :]
    w = weight[...]
    adjoint_product(ids, parts, w * w * (observed[...] - q), out, first, second)
    aux_rows(out)


def rhs_kernel(ids, parts, ga, gb, scale, out, resid, first, second):
    rhs = scale[...] * (ga[:128, :] + gb[:128, :])
    resid[...] = rhs
    forward_product(ids, parts, scale[...] * rhs, out, first, second)
    aux_rows(out, column_sum(rhs * rhs))


def push_values(q0, q1, q2, q3, weight, pushed, scal):
    t = q0[:128, :] + q1[:128, :] + q2[:128, :] + q3[:128, :]
    sums = q0[128:ROWS, :] + q1[128:ROWS, :] + q2[128:ROWS, :] + q3[128:ROWS, :]
    rr = total(sums[0:1, :]) + jnp.zeros((1, BS), F32)
    if pushed is None:
        beta, dd, q = jnp.zeros((1, BS), F32), rr, t
    else:
        rd = total(sums[1:2, :])
        beta = rr / scal[0:1, :]
        dd = rr + 2.0 * beta * rd + beta * beta * scal[1:2, :]
        q = t + beta * pushed[...]
    w = weight[...]
    u = w * w * q
    return rr, dd, beta, q, u


def store_scalars(scal_out, rr, dd, beta):
    scal_out[...] = jnp.zeros((8, BS), F32)
    scal_out[0:1, :] = rr
    scal_out[1:2, :] = dd
    scal_out[2:3, :] = beta


def push_kernel(first_turn, ids, parts, q0, q1, q2, q3, weight, *refs):
    if first_turn:
        pushed = scal = None
    else:
        pushed, scal, *refs = refs
    out, q_out, scal_out, first, second = refs
    rr, dd, beta, q, u = push_values(q0, q1, q2, q3, weight, pushed, scal)
    q_out[...] = q
    store_scalars(scal_out, rr, dd, beta)
    adjoint_product(ids, parts, u, out, first, second)
    aux_rows(out, column_sum(u * q))


def last_push_kernel(q0, q1, q2, q3, weight, pushed, scal, out, scal_out):
    rr, dd, beta, q, u = push_values(q0, q1, q2, q3, weight, pushed, scal)
    store_scalars(scal_out, rr, dd, beta)
    out[...] = jnp.zeros((8, BS), F32)
    out[0:1, :] = column_sum(u * q)


def turn_kernel(first_turn, ids, parts, ga, gb, scale, band, scal, resid, *refs):
    if first_turn:
        out, resid_out, direction_out, step_out, first, second = refs
        direction, step = jnp.zeros((128, BS), F32), jnp.zeros((128, BS), F32)
    else:
        direction, step, out, resid_out, direction_out, step_out, first, second = refs
        direction, step = direction[...], step[...]
    d, alpha = newton_direction(ga[128:129, :], gb[128:129, :], resid[...], direction, scal[...])
    image = scale[...] * (ga[:128, :] + gb[:128, :]) + 0.05 * band[...] * d
    r = resid[...] - alpha * image
    direction_out[...] = d
    step_out[...] = step + alpha * d
    resid_out[...] = r
    forward_product(ids, parts, scale[...] * r, out, first, second)
    aux_rows(out, column_sum(r * r), column_sum(r * d))


def per_device(
    sens_blocks, block_rows, block_cols, block_count, band_mask, level_set, observed, data_weight
):
    row_ids, col_ids = block_rows.reshape(-1), block_cols.reshape(-1)
    count = block_count.reshape(1)
    live = jnp.arange(SLOTS, dtype=jnp.int32) < count[0]
    row_to, col_to = jnp.where(live, row_ids, TRASH), jnp.where(live, col_ids, TRASH)
    ids = jnp.concatenate([row_to, col_ids, row_ids, col_to, count])
    band = band_mask.astype(F32).reshape(128, BS)
    phi = level_set.reshape(128, BS)
    obs, weight = observed.reshape(128, BS), data_weight.reshape(128, BS)
    parts, flipped = split_blocks(ids, sens_blocks.reshape(SLOTS, BS, BS))
    wide, plain, small = (pltpu.VMEM((n, BS), F32) for n in (ROWS, 128, 8))

    def product(kernel, forward, operands, outs, name):
        return pl.pallas_call(
            kernel,
            out_shape=outs,
            in_specs=[SMEM] + [VMEM] * (1 + len(operands)),
            out_specs=[VMEM] * len(outs),
            scratch_shapes=TILES,
            compiler_params=PARAMS,
            name=name,
        )(ids, flipped if forward else parts, *operands)

    def exchange(value, axis, inner, along_outer):
        outer = 4
        shifts = range(1, outer if along_outer else inner)
        got = [value]
        for s in shifts:
            if along_outer:
                pairs = [(a * inner + b, (a + s) % outer * inner + b) for a in range(outer) for b in range(inner)]
            else:
                pairs = [(a * inner + b, a * inner + (b + s) % inner) for a in range(outer) for b in range(inner)]
            got.append(lax.ppermute(value, axis, pairs))
        return got

    def over_col(value):
        z = exchange(value, "col", 4, True)
        return exchange(z[0] + z[1] + z[2] + z[3], "col", 4, False)

    def over_row(value):
        y = exchange(value, "row", 2, True)
        return exchange(y[0] + y[1] + y[2] + y[3], "row", 2, False)

    def start(update):
        if update is None:
            out, scale = product(
                lambda *r: start_kernel(False, *r), True, (phi, band), [wide, plain], "start"
            )
            return out, scale, phi
        return product(
            lambda *r: start_kernel(True, *r), True, (*update, band), [wide, plain, plain], "restart"
        )

    update = None
    for outer in range(GN_ITERS):
        out, scale, phi = start(update)
        (out,) = product(misfit_kernel, False, (*over_col(out), obs, weight), [wide], "misfit")
        out, resid = product(rhs_kernel, True, (*over_row(out), scale), [wide, plain], "rhs")
        state, pushed = (), ()
        for turn in range(CG_ITERS - 1):
            out, q, scal = product(
                lambda *r, one=turn == 0: push_kernel(one, *r),
                False,
                (*over_col(out), weight, *pushed),
                [wide, plain, small],
                "push",
            )
            pushed = (q, scal)
            out, resid, direction, step = product(
                lambda *r, one=turn == 0: turn_kernel(one, *r),
                True,
                (*over_row(out), scale, band, scal, resid, *state),
                [wide, plain, plain, plain],
                "turn",
            )
            state = (direction, step)
        sums, scal = pl.pallas_call(
            last_push_kernel,
            out_shape=[small, small],
            in_specs=[VMEM] * 7,
            out_specs=[VMEM] * 2,
            compiler_params=PARAMS,
            name="last_push",
        )(*over_col(out), weight, *pushed)
        update = (phi, *over_row(sums), resid, direction, step, scal)
    out, _, phi = start(update)
    q = over_col(out)
    misfit = weight * (obs - (q[0] + q[1] + q[2] + q[3])[:128])
    return phi.reshape(-1), misfit.reshape(-1)


def solution(mesh):
    return jax.shard_map(
        per_device,
        mesh=mesh,
        in_specs=(
            P("row", "col", None, None),
            P("row", "col"),
            P("row", "col"),
            P("row", "col"),
            P("col"),
            P("col"),
            P("row"),
            P("row"),
        ),
        out_specs=(P("col"), P("row")),
        check_vma=False,
    )
```

```python
import jax
import jax.numpy as jnp
from jax import lax
from jax.experimental import pallas as pl
from jax.experimental.pallas import tpu as pltpu
from jax.sharding import PartitionSpec as P

BS = 128
GN_ITERS = 2
CG_ITERS = 4
SLOTS = 192
GROUP = 48
CHUNK = 16
ROWS = 136
F32, BF16 = jnp.float32, jnp.bfloat16

VMEM = pl.BlockSpec(memory_space=pltpu.VMEM)
SMEM = pl.BlockSpec(memory_space=pltpu.SMEM)
PARAMS = pltpu.CompilerParams(vmem_limit_bytes=16 << 20)
TILES = [pltpu.VMEM((128, 16, 128), BF16), pltpu.VMEM((128, 16, 128), BF16)]


def groups(count):
    return (count[0] + GROUP - 1) // GROUP


def split_kernel(count_in, rows_in, cols_in, sens, parts, flipped, count, rows, cols, buf, sem, ids_sem):
    chunks = groups(count_in) * (GROUP // CHUNK)
    live = count_in[0]
    count[0] = live
    row_copy = pltpu.make_async_copy(rows_in, rows, ids_sem.at[0])
    col_copy = pltpu.make_async_copy(cols_in, cols, ids_sem.at[1])
    row_copy.start()
    col_copy.start()

    def copy(g):
        at = pl.ds(g * CHUNK, CHUNK)
        return pltpu.make_async_copy(sens.at[at], buf.at[at], sem.at[g])

    def begin(g, carry):
        copy(g).start()
        return carry

    def body(g, carry):
        copy(g).wait()
        for b in range(CHUNK):
            k = g * CHUNK + b
            value = jnp.where(k < live, buf[k], 0.0)
            for to, v in ((parts, value), (flipped, value.T)):
                high = v.astype(BF16)
                to[k, :, :BS] = high
                to[k, :, BS:] = (v - high.astype(F32)).astype(BF16)
        return carry

    lax.fori_loop(0, chunks, begin, 0)
    lax.fori_loop(0, chunks, body, 0)
    row_copy.wait()
    col_copy.wait()


def split_blocks(count, rows, cols, sens):
    halves = pltpu.VMEM((SLOTS, BS, 2 * BS), BF16)
    hbm = pl.BlockSpec(memory_space=pltpu.HBM)
    return pl.pallas_call(
        split_kernel,
        out_shape=[halves, halves]
        + [pltpu.SMEM((n,), jnp.int32) for n in (1, SLOTS, SLOTS)],
        in_specs=[SMEM, hbm, hbm, hbm],
        out_specs=[VMEM, VMEM, SMEM, SMEM, SMEM],
        scratch_shapes=[
            pltpu.VMEM((SLOTS, BS, BS), F32),
            pltpu.SemaphoreType.DMA((SLOTS // CHUNK,)),
            pltpu.SemaphoreType.DMA((2,)),
        ],
        compiler_params=PARAMS,
        name="split_blocks",
    )(count, *(pltpu.with_memory_space_constraint(v, pltpu.HBM) for v in (rows, cols, sens)))


def fill_tiles(x, first, second):
    high = x.astype(BF16).astype(F32)
    low = x - high
    at = lax.broadcasted_iota(jnp.int32, (128, 16, BS), 1)
    high, low = high[:, None, :], low[:, None, :]
    first[...] = jnp.where(at == 0, high, jnp.where(at == 1, low, 0.0)).astype(BF16)
    second[...] = jnp.where(at == 2, high, jnp.where(at == 3, low, 0.0)).astype(BF16)


def product_of(count, source, target, parts, x, out, first, second):
    fill_tiles(x, first, second)
    out[...] = jnp.zeros_like(out)

    def body(g, carry):
        for p in range(0, GROUP, 2):
            k = g * GROUP + p
            r = lax.dot_general(
                jnp.concatenate([first[source[k]], second[source[k + 1]]], axis=1),
                parts[pl.ds(k, 2)].reshape(2 * BS, 2 * BS),
                (((1,), (0,)), ((), ())),
                preferred_element_type=F32,
            )
            r = r[0:8, :BS] + r[0:8, BS:]
            out[pl.ds(target[k], 1), :] += r[0:1] + r[1:2]
            out[pl.ds(target[k + 1], 1), :] += r[2:3] + r[3:4]
        return carry

    lax.fori_loop(0, groups(count), body, 0)


def forward_product(count, rows, cols, flipped, x, out, first, second):
    product_of(count, cols, rows, flipped, x, out, first, second)


def adjoint_product(count, rows, cols, parts, x, out, first, second):
    product_of(count, rows, cols, parts, x, out, first, second)


def aux_rows(out, *vectors):
    out[128:ROWS, :] = jnp.zeros((8, BS), F32)
    for i, v in enumerate(vectors):
        out[128 + i : 129 + i, :] = v


def column_sum(x):
    return jnp.sum(x, axis=0, keepdims=True)


def total(row):
    return jnp.sum(row, axis=1, keepdims=True)


def newton_direction(ga, gb, resid, direction, scal):
    d = resid + scal[2:3, :] * direction
    alpha = scal[0:1, :] / (total(ga + gb) + 0.05 * scal[1:2, :])
    return d, alpha


def start_kernel(with_update, count, rows, cols, parts, *refs):
    if with_update:
        phi, sa, sb, resid, direction, step, scal, band, out, scale, phi_out, first, second = refs
        d, alpha = newton_direction(sa[0:1, :], sb[0:1, :], resid[...], direction[...], scal[...])
        level = phi[...] + (step[...] + alpha * d)
        phi_out[...] = level
    else:
        phi, band, out, scale, first, second = refs
        level = phi[...]
    heavy = jax.nn.sigmoid(level / 0.5)
    scale[...] = band[...].astype(F32) * heavy * (1.0 - heavy) / 0.5
    forward_product(count, rows, cols, parts, heavy, out, first, second)
    aux_rows(out)


def misfit_kernel(count, rows, cols, parts, q0, q1, q2, q3, observed, weight, out, first, second):
    q = q0[:128, :] + q1[:128, :] + q2[:128, :] + q3[:128, :]
    w = weight[...]
    adjoint_product(count, rows, cols, parts, w * w * (observed[...] - q), out, first, second)
    aux_rows(out)


def rhs_kernel(count, rows, cols, parts, ga, gb, scale, out, resid, first, second):
    rhs = scale[...] * (ga[:128, :] + gb[:128, :])
    resid[...] = rhs
    forward_product(count, rows, cols, parts, scale[...] * rhs, out, first, second)
    aux_rows(out, column_sum(rhs * rhs))


def push_values(q0, q1, q2, q3, weight, pushed, scal):
    t = q0[:128, :] + q1[:128, :] + q2[:128, :] + q3[:128, :]
    sums = q0[128:ROWS, :] + q1[128:ROWS, :] + q2[128:ROWS, :] + q3[128:ROWS, :]
    rr = total(sums[0:1, :]) + jnp.zeros((1, BS), F32)
    if pushed is None:
        beta, dd, q = jnp.zeros((1, BS), F32), rr, t
    else:
        rd = total(sums[1:2, :])
        beta = rr / scal[0:1, :]
        dd = rr + 2.0 * beta * rd + beta * beta * scal[1:2, :]
        q = t + beta * pushed[...]
    w = weight[...]
    u = w * w * q
    return rr, dd, beta, q, u


def store_scalars(scal_out, rr, dd, beta):
    scal_out[...] = jnp.zeros((8, BS), F32)
    scal_out[0:1, :] = rr
    scal_out[1:2, :] = dd
    scal_out[2:3, :] = beta


def push_kernel(first_turn, count, rows, cols, parts, q0, q1, q2, q3, weight, *refs):
    if first_turn:
        pushed = scal = None
    else:
        pushed, scal, *refs = refs
    out, q_out, scal_out, first, second = refs
    rr, dd, beta, q, u = push_values(q0, q1, q2, q3, weight, pushed, scal)
    q_out[...] = q
    store_scalars(scal_out, rr, dd, beta)
    adjoint_product(count, rows, cols, parts, u, out, first, second)
    aux_rows(out, column_sum(u * q))


def last_push_kernel(q0, q1, q2, q3, weight, pushed, scal, out, scal_out):
    rr, dd, beta, q, u = push_values(q0, q1, q2, q3, weight, pushed, scal)
    store_scalars(scal_out, rr, dd, beta)
    out[...] = jnp.zeros((8, BS), F32)
    out[0:1, :] = column_sum(u * q)


def turn_kernel(first_turn, count, rows, cols, parts, ga, gb, scale, band, scal, resid, *refs):
    if first_turn:
        out, resid_out, direction_out, step_out, first, second = refs
        direction, step = jnp.zeros((128, BS), F32), jnp.zeros((128, BS), F32)
    else:
        direction, step, out, resid_out, direction_out, step_out, first, second = refs
        direction, step = direction[...], step[...]
    d, alpha = newton_direction(ga[128:129, :], gb[128:129, :], resid[...], direction, scal[...])
    image = scale[...] * (ga[:128, :] + gb[:128, :]) + 0.05 * band[...].astype(F32) * d
    r = resid[...] - alpha * image
    direction_out[...] = d
    step_out[...] = step + alpha * d
    resid_out[...] = r
    forward_product(count, rows, cols, parts, scale[...] * r, out, first, second)
    aux_rows(out, column_sum(r * r), column_sum(r * d))


def per_device(
    sens_blocks, block_rows, block_cols, block_count, band_mask, level_set, observed, data_weight
):
    band = band_mask.reshape(128, BS)
    phi = level_set.reshape(128, BS)
    obs, weight = observed.reshape(128, BS), data_weight.reshape(128, BS)
    parts, flipped, *tables = split_blocks(
        block_count.reshape(1),
        block_rows.reshape(-1),
        block_cols.reshape(-1),
        sens_blocks.reshape(SLOTS, BS, BS),
    )
    tables = [pltpu.with_memory_space_constraint(t, pltpu.SMEM) for t in tables]
    wide, plain, small = (pltpu.VMEM((n, BS), F32) for n in (ROWS, 128, 8))

    def product(kernel, forward, operands, outs, name):
        return pl.pallas_call(
            kernel,
            out_shape=outs,
            in_specs=[SMEM] * 3 + [VMEM] * (1 + len(operands)),
            out_specs=[VMEM] * len(outs),
            scratch_shapes=TILES,
            compiler_params=PARAMS,
            name=name,
        )(*tables, flipped if forward else parts, *operands)

    def exchange(value, axis, size, partners):
        return [value] + [lax.ppermute(value, axis, [(i, i ^ p) for i in range(size)]) for p in partners]

    def over_col(value):
        z = exchange(value, "col", 16, (4, 12, 8))
        return exchange(z[0] + z[1] + z[2] + z[3], "col", 16, (1, 3, 2))

    def over_row(value):
        y = exchange(value, "row", 8, (2, 6, 4))
        return exchange(y[0] + y[1] + y[2] + y[3], "row", 8, (1,))

    def start(update):
        if update is None:
            out, scale = product(
                lambda *r: start_kernel(False, *r), True, (phi, band), [wide, plain], "start"
            )
            return out, scale, phi
        return product(
            lambda *r: start_kernel(True, *r), True, (*update, band), [wide, plain, plain], "restart"
        )

    update = None
    for outer in range(GN_ITERS):
        out, scale, phi = start(update)
        (out,) = product(misfit_kernel, False, (*over_col(out), obs, weight), [wide], "misfit")
        out, resid = product(rhs_kernel, True, (*over_row(out), scale), [wide, plain], "rhs")
        state, pushed = (), ()
        for turn in range(CG_ITERS - 1):
            out, q, scal = product(
                lambda *r, one=turn == 0: push_kernel(one, *r),
                False,
                (*over_col(out), weight, *pushed),
                [wide, plain, small],
                "push",
            )
            pushed = (q, scal)
            out, resid, direction, step = product(
                lambda *r, one=turn == 0: turn_kernel(one, *r),
                True,
                (*over_row(out), scale, band, scal, resid, *state),
                [wide, plain, plain, plain],
                "turn",
            )
            state = (direction, step)
        sums, scal = pl.pallas_call(
            last_push_kernel,
            out_shape=[small, small],
            in_specs=[VMEM] * 7,
            out_specs=[VMEM] * 2,
            compiler_params=PARAMS,
            name="last_push",
        )(*over_col(out), weight, *pushed)
        update = (phi, *over_row(sums), resid, direction, step, scal)
    out, _, phi = start(update)
    q = over_col(out)
    misfit = weight * (obs - (q[0] + q[1] + q[2] + q[3])[:128])
    return phi.reshape(-1), misfit.reshape(-1)


def solution(mesh):
    return jax.shard_map(
        per_device,
        mesh=mesh,
        in_specs=(
            P("row", "col", None, None),
            P("row", "col"),
            P("row", "col"),
            P("row", "col"),
            P("col"),
            P("col"),
            P("row"),
            P("row"),
        ),
        out_specs=(P("col"), P("row")),
        check_vma=False,
    )
```

```python
import jax
import jax.numpy as jnp
from jax import lax
from jax.experimental import pallas as pl
from jax.experimental.pallas import tpu as pltpu
from jax.sharding import PartitionSpec as P

BS = 128
GN_ITERS = 2
CG_ITERS = 4
SLOTS = 192
GROUP = 96
CHUNK = 16
ROWS = 136
F32, BF16 = jnp.float32, jnp.bfloat16

VMEM = pl.BlockSpec(memory_space=pltpu.VMEM)
SMEM = pl.BlockSpec(memory_space=pltpu.SMEM)
PARAMS = pltpu.CompilerParams(vmem_limit_bytes=16 << 20)
TILES = [pltpu.VMEM((128, 16, 128), BF16), pltpu.VMEM((128, 16, 128), BF16)]


def groups(count):
    return (count[0] + GROUP - 1) // GROUP


def split_kernel(count_in, rows_in, cols_in, sens, parts, flipped, count, rows, cols, buf, sem, ids_sem):
    live = count_in[0, 0]
    chunks = (live + CHUNK - 1) // CHUNK
    count[0] = live
    row_copy = pltpu.make_async_copy(rows_in, rows, ids_sem.at[0])
    col_copy = pltpu.make_async_copy(cols_in, cols, ids_sem.at[1])
    row_copy.start()
    col_copy.start()

    def copy(g):
        at = pl.ds(g * CHUNK, CHUNK)
        return pltpu.make_async_copy(sens.at[at], buf.at[at], sem.at[g])

    def begin(g, carry):
        copy(g).start()
        return carry

    def body(g, carry):
        copy(g).wait()
        for b in range(CHUNK):
            k = g * CHUNK + b
            value = jnp.where(k < live, buf[k], 0.0)
            for to, v in ((parts, value), (flipped, value.T)):
                high = v.astype(BF16)
                to[k, :, :BS] = high
                to[k, :, BS:] = (v - high.astype(F32)).astype(BF16)
        return carry

    def clear(g, carry):
        at = pl.ds(g * CHUNK, CHUNK)
        parts[at] = jnp.zeros((CHUNK, BS, 2 * BS), BF16)
        flipped[at] = jnp.zeros((CHUNK, BS, 2 * BS), BF16)
        return carry

    lax.fori_loop(0, chunks, begin, 0)
    lax.fori_loop(chunks, groups(count) * (GROUP // CHUNK), clear, 0)
    lax.fori_loop(0, chunks, body, 0)
    row_copy.wait()
    col_copy.wait()


def split_blocks(count, rows, cols, sens):
    halves = pltpu.VMEM((SLOTS, BS, 2 * BS), BF16)
    hbm = pl.BlockSpec(memory_space=pltpu.HBM)
    return pl.pallas_call(
        split_kernel,
        out_shape=[halves, halves]
        + [pltpu.SMEM((n,), jnp.int32) for n in (1, SLOTS, SLOTS)],
        in_specs=[SMEM, hbm, hbm, hbm],
        out_specs=[VMEM, VMEM, SMEM, SMEM, SMEM],
        scratch_shapes=[
            pltpu.VMEM((SLOTS, BS, BS), F32),
            pltpu.SemaphoreType.DMA((SLOTS // CHUNK,)),
            pltpu.SemaphoreType.DMA((2,)),
        ],
        compiler_params=PARAMS,
        name="split_blocks",
    )(count, *(pltpu.with_memory_space_constraint(v, pltpu.HBM) for v in (rows, cols, sens)))


def fill_tiles(x, first, second):
    high = x.astype(BF16).astype(F32)
    low = x - high
    at = lax.broadcasted_iota(jnp.int32, (128, 8, BS), 1)
    high, low = high[:, None, :], low[:, None, :]
    for to, row in ((first, 0), (second, 2)):
        tile = jnp.where(at == row, high, jnp.where(at == row + 1, low, 0.0))
        to[...] = jnp.concatenate([tile, tile], axis=1).astype(BF16)


def product_of(count, source, target, parts, x, out, first, second):
    fill_tiles(x, first, second)
    out[...] = jnp.zeros_like(out)

    def body(g, carry):
        for p in range(0, GROUP, 2):
            k = g * GROUP + p
            r = lax.dot_general(
                jnp.concatenate([first[source[k]], second[source[k + 1]]], axis=1),
                parts[pl.ds(k, 2)].reshape(2 * BS, 2 * BS),
                (((1,), (0,)), ((), ())),
                preferred_element_type=F32,
            )
            r = r[0:8, :BS] + r[0:8, BS:]
            out[pl.ds(target[k], 1), :] += r[0:1] + r[1:2]
            out[pl.ds(target[k + 1], 1), :] += r[2:3] + r[3:4]
        return carry

    lax.fori_loop(0, groups(count), body, 0)


def forward_product(count, rows, cols, flipped, x, out, first, second):
    product_of(count, cols, rows, flipped, x, out, first, second)


def adjoint_product(count, rows, cols, parts, x, out, first, second):
    product_of(count, rows, cols, parts, x, out, first, second)


def aux_rows(out, *vectors):
    out[128:ROWS, :] = jnp.zeros((8, BS), F32)
    for i, v in enumerate(vectors):
        out[128 + i : 129 + i, :] = v


def column_sum(x):
    return jnp.sum(x, axis=0, keepdims=True)


def total(row):
    return jnp.sum(row, axis=1, keepdims=True)


def newton_direction(ga, gb, resid, direction, scal):
    d = resid + scal[2:3, :] * direction
    alpha = scal[0:1, :] / (total(ga + gb) + 0.05 * scal[1:2, :])
    return d, alpha


def start_kernel(count, rows, cols, parts, phi, band, out, scale, first, second):
    heavy = jax.nn.sigmoid(phi[...] / 0.5)
    scale[...] = band[...].astype(F32) * heavy * (1.0 - heavy) / 0.5
    forward_product(count, rows, cols, parts, heavy, out, first, second)
    aux_rows(out)


def restart_kernel(final, count, rows, cols, parts, phi, sa, sb, resid, direction, step, scal, *refs):
    if final:
        out, phi_out, first, second = refs
    else:
        band, out, phi_out, scale, first, second = refs
    d, alpha = newton_direction(sa[0:1, :], sb[0:1, :], resid[...], direction[...], scal[...])
    level = phi[...] + (step[...] + alpha * d)
    phi_out[...] = level
    heavy = jax.nn.sigmoid(level / 0.5)
    if not final:
        scale[...] = band[...].astype(F32) * heavy * (1.0 - heavy) / 0.5
    forward_product(count, rows, cols, parts, heavy, out, first, second)
    aux_rows(out)


def misfit_kernel(count, rows, cols, parts, q0, q1, q2, q3, observed, weight, out, first, second):
    q = q0[:128, :] + q1[:128, :] + q2[:128, :] + q3[:128, :]
    w = weight[...]
    adjoint_product(count, rows, cols, parts, w * w * (observed[...] - q), out, first, second)
    aux_rows(out)


def rhs_kernel(count, rows, cols, parts, ga, gb, scale, out, resid, first, second):
    rhs = scale[...] * (ga[:128, :] + gb[:128, :])
    resid[...] = rhs
    forward_product(count, rows, cols, parts, scale[...] * rhs, out, first, second)
    aux_rows(out, column_sum(rhs * rhs))


def push_values(q0, q1, q2, q3, weight, pushed, scal):
    t = q0[:128, :] + q1[:128, :] + q2[:128, :] + q3[:128, :]
    sums = q0[128:ROWS, :] + q1[128:ROWS, :] + q2[128:ROWS, :] + q3[128:ROWS, :]
    rr = total(sums[0:1, :]) + jnp.zeros((1, BS), F32)
    if pushed is None:
        beta, dd, q = jnp.zeros((1, BS), F32), rr, t
    else:
        rd = total(sums[1:2, :])
        beta = rr / scal[0:1, :]
        dd = rr + 2.0 * beta * rd + beta * beta * scal[1:2, :]
        q = t + beta * pushed[...]
    w = weight[...]
    u = w * w * q
    return rr, dd, beta, q, u


def store_scalars(scal_out, rr, dd, beta):
    scal_out[...] = jnp.zeros((8, BS), F32)
    scal_out[0:1, :] = rr
    scal_out[1:2, :] = dd
    scal_out[2:3, :] = beta


def push_kernel(first_turn, count, rows, cols, parts, q0, q1, q2, q3, weight, *refs):
    if first_turn:
        pushed = scal = None
    else:
        pushed, scal, *refs = refs
    out, q_out, scal_out, first, second = refs
    rr, dd, beta, q, u = push_values(q0, q1, q2, q3, weight, pushed, scal)
    q_out[...] = q
    store_scalars(scal_out, rr, dd, beta)
    adjoint_product(count, rows, cols, parts, u, out, first, second)
    aux_rows(out, column_sum(u * q))


def last_push_kernel(q0, q1, q2, q3, weight, pushed, scal, out, scal_out):
    rr, dd, beta, q, u = push_values(q0, q1, q2, q3, weight, pushed, scal)
    store_scalars(scal_out, rr, dd, beta)
    out[...] = jnp.zeros((8, BS), F32)
    out[0:1, :] = column_sum(u * q)


def turn_kernel(first_turn, count, rows, cols, parts, ga, gb, scale, band, scal, resid, *refs):
    if first_turn:
        out, resid_out, direction_out, step_out, first, second = refs
        direction, step = jnp.zeros((128, BS), F32), jnp.zeros((128, BS), F32)
    else:
        direction, step, out, resid_out, direction_out, step_out, first, second = refs
        direction, step = direction[...], step[...]
    d, alpha = newton_direction(ga[128:129, :], gb[128:129, :], resid[...], direction, scal[...])
    image = scale[...] * (ga[:128, :] + gb[:128, :]) + 0.05 * band[...].astype(F32) * d
    r = resid[...] - alpha * image
    direction_out[...] = d
    step_out[...] = step + alpha * d
    resid_out[...] = r
    forward_product(count, rows, cols, parts, scale[...] * r, out, first, second)
    aux_rows(out, column_sum(r * r), column_sum(r * d))


def per_device(
    sens_blocks, block_rows, block_cols, block_count, band_mask, level_set, observed, data_weight
):
    band = band_mask.reshape(128, BS)
    phi = level_set.reshape(128, BS)
    obs, weight = observed.reshape(128, BS), data_weight.reshape(128, BS)
    parts, flipped, *tables = split_blocks(
        block_count,
        block_rows.reshape(-1),
        block_cols.reshape(-1),
        sens_blocks.reshape(SLOTS, BS, BS),
    )
    tables = [pltpu.with_memory_space_constraint(t, pltpu.SMEM) for t in tables]
    wide, plain, small = (pltpu.VMEM((n, BS), F32) for n in (ROWS, 128, 8))

    def product(kernel, forward, operands, outs, name):
        return pl.pallas_call(
            kernel,
            out_shape=outs,
            in_specs=[SMEM] * 3 + [VMEM] * (1 + len(operands)),
            out_specs=[VMEM] * len(outs),
            scratch_shapes=TILES,
            compiler_params=PARAMS,
            name=name,
        )(*tables, flipped if forward else parts, *operands)

    def exchange(value, axis, size, partners):
        return [value] + [lax.ppermute(value, axis, [(i, i ^ p) for i in range(size)]) for p in partners]

    def over_col(value):
        z = exchange(value, "col", 16, (4, 12, 8))
        return exchange(z[0] + z[1] + z[2] + z[3], "col", 16, (1, 3, 2))

    def over_row(value):
        swap = [(i, i ^ 1) for i in range(8)]
        chip = value + lax.ppermute(value, "row", swap)
        far = lax.ppermute(chip, "row", [(i, i ^ 4) for i in range(8)])
        near = lax.ppermute(chip, "row", [(i, i ^ (6 if i % 2 else 2)) for i in range(8)])
        other = lax.ppermute(near, "row", swap)
        return chip + near + far, other

    update = None
    for outer in range(GN_ITERS):
        if update is None:
            out, scale = product(start_kernel, True, (phi, band), [wide, plain], "start")
        else:
            out, phi, scale = product(
                lambda *r: restart_kernel(False, *r), True, (*update, band), [wide, plain, plain], "restart"
            )
        (out,) = product(misfit_kernel, False, (*over_col(out), obs, weight), [wide], "misfit")
        out, resid = product(rhs_kernel, True, (*over_row(out), scale), [wide, plain], "rhs")
        state, pushed = (), ()
        for turn in range(CG_ITERS - 1):
            out, q, scal = product(
                lambda *r, one=turn == 0: push_kernel(one, *r),
                False,
                (*over_col(out), weight, *pushed),
                [wide, plain, small],
                "push",
            )
            pushed = (q, scal)
            out, resid, direction, step = product(
                lambda *r, one=turn == 0: turn_kernel(one, *r),
                True,
                (*over_row(out), scale, band, scal, resid, *state),
                [wide, plain, plain, plain],
                "turn",
            )
            state = (direction, step)
        sums, scal = pl.pallas_call(
            last_push_kernel,
            out_shape=[small, small],
            in_specs=[VMEM] * 7,
            out_specs=[VMEM] * 2,
            compiler_params=PARAMS,
            name="last_push",
        )(*over_col(out), weight, *pushed)
        update = (phi, *over_row(sums), resid, direction, step, scal)
    out, phi = product(lambda *r: restart_kernel(True, *r), True, update, [wide, plain], "final")
    q = over_col(out)
    misfit = weight * (obs - (q[0] + q[1] + q[2] + q[3])[:128])
    return phi.reshape(-1), misfit.reshape(-1)


def solution(mesh):
    return jax.shard_map(
        per_device,
        mesh=mesh,
        in_specs=(
            P("row", "col", None, None),
            P("row", "col"),
            P("row", "col"),
            P("row", "col"),
            P("col"),
            P("col"),
            P("row"),
            P("row"),
        ),
        out_specs=(P("col"), P("row")),
        check_vma=False,
    )
```

```python
import jax
import jax.numpy as jnp
from jax import lax
from jax.experimental import pallas as pl
from jax.experimental.pallas import tpu as pltpu
from jax.sharding import PartitionSpec as P

BS = 128
GN_ITERS = 2
CG_ITERS = 4
SLOTS = 192
GROUP = 96
CHUNK = 16
ROWS = 136
F32, BF16 = jnp.float32, jnp.bfloat16

VMEM = pl.BlockSpec(memory_space=pltpu.VMEM)
SMEM = pl.BlockSpec(memory_space=pltpu.SMEM)
PARAMS = pltpu.CompilerParams(vmem_limit_bytes=16 << 20)
TILES = [pltpu.VMEM((128, 16, 128), BF16), pltpu.VMEM((128, 16, 128), BF16), pltpu.VMEM((128, BS), F32)]


def groups(count):
    return (count[0] + GROUP - 1) // GROUP


def split_kernel(count_in, rows_in, cols_in, sens, parts, flipped, count, rows, cols, buf, sem, ids_sem):
    live = count_in[0, 0]
    chunks = (live + CHUNK - 1) // CHUNK
    count[0] = live
    row_copy = pltpu.make_async_copy(rows_in, rows, ids_sem.at[0])
    col_copy = pltpu.make_async_copy(cols_in, cols, ids_sem.at[1])
    row_copy.start()
    col_copy.start()

    def copy(g):
        at = pl.ds(g * CHUNK, CHUNK)
        return pltpu.make_async_copy(sens.at[at], buf.at[at], sem.at[g])

    def begin(g, carry):
        copy(g).start()
        return carry

    def body(g, carry):
        copy(g).wait()
        for b in range(CHUNK):
            k = g * CHUNK + b
            value = jnp.where(k < live, buf[k], 0.0)
            for to, v in ((parts, value), (flipped, value.T)):
                high = v.astype(BF16)
                to[k, :, :BS] = high
                to[k, :, BS:] = (v - high.astype(F32)).astype(BF16)
        return carry

    def clear(g, carry):
        at = pl.ds(g * CHUNK, CHUNK)
        parts[at] = jnp.zeros((CHUNK, BS, 2 * BS), BF16)
        flipped[at] = jnp.zeros((CHUNK, BS, 2 * BS), BF16)
        return carry

    lax.fori_loop(0, chunks, begin, 0)
    lax.fori_loop(chunks, groups(count) * (GROUP // CHUNK), clear, 0)
    lax.fori_loop(0, chunks, body, 0)
    row_copy.wait()
    col_copy.wait()


def split_blocks(count, rows, cols, sens):
    halves = pltpu.VMEM((SLOTS, BS, 2 * BS), BF16)
    hbm = pl.BlockSpec(memory_space=pltpu.HBM)
    return pl.pallas_call(
        split_kernel,
        out_shape=[halves, halves]
        + [pltpu.SMEM((n,), jnp.int32) for n in (1, SLOTS, SLOTS)],
        in_specs=[SMEM, hbm, hbm, hbm],
        out_specs=[VMEM, VMEM, SMEM, SMEM, SMEM],
        scratch_shapes=[
            pltpu.VMEM((SLOTS, BS, BS), F32),
            pltpu.SemaphoreType.DMA((SLOTS // CHUNK,)),
            pltpu.SemaphoreType.DMA((2,)),
        ],
        compiler_params=PARAMS,
        name="split_blocks",
    )(count, *(pltpu.with_memory_space_constraint(v, pltpu.HBM) for v in (rows, cols, sens)))


def fill_tiles(x, first, second):
    high = x.astype(BF16).astype(F32)
    low = x - high
    at = lax.broadcasted_iota(jnp.int32, (128, 8, BS), 1)
    high, low = high[:, None, :], low[:, None, :]
    for to, row in ((first, 0), (second, 2)):
        tile = jnp.where(at == row, high, jnp.where(at == row + 1, low, 0.0))
        to[...] = jnp.concatenate([tile, tile], axis=1).astype(BF16)


def product_of(count, source, target, parts, x, out, first, second, values):
    fill_tiles(x, first, second)
    values[...] = x
    out[...] = jnp.zeros_like(out)

    def matrix_pair(k):
        r = lax.dot_general(
            jnp.concatenate([first[source[k]], second[source[k + 1]]], axis=1),
            parts[pl.ds(k, 2)].reshape(2 * BS, 2 * BS),
            (((1,), (0,)), ((), ())),
            preferred_element_type=F32,
        )
        r = r[0:8, :BS] + r[0:8, BS:]
        out[pl.ds(target[k], 1), :] += r[0:1] + r[1:2]
        out[pl.ds(target[k + 1], 1), :] += r[2:3] + r[3:4]

    def vector_block(k):
        weights = jnp.broadcast_to(values[pl.ds(source[k], 1), :], (BS, BS)).T
        block = parts[k]
        terms = (block[:, :BS].astype(F32) + block[:, BS:].astype(F32)) * weights
        terms = jnp.sum(terms.reshape(BS // 8, 8, BS), axis=0)
        out[pl.ds(target[k], 1), :] += jnp.sum(terms, axis=0, keepdims=True)

    def body(g, carry):
        for at in range(0, GROUP, 16):
            k = g * GROUP + at
            for p in range(0, 10, 2):
                matrix_pair(k + p)
            for p in range(10, 16):
                vector_block(k + p)
        return carry

    lax.fori_loop(0, groups(count), body, 0)


def forward_product(count, rows, cols, flipped, x, out, first, second, values):
    product_of(count, cols, rows, flipped, x, out, first, second, values)


def adjoint_product(count, rows, cols, parts, x, out, first, second, values):
    product_of(count, rows, cols, parts, x, out, first, second, values)


def aux_rows(out, *vectors):
    out[128:ROWS, :] = jnp.zeros((8, BS), F32)
    for i, v in enumerate(vectors):
        out[128 + i : 129 + i, :] = v


def column_sum(x):
    return jnp.sum(x, axis=0, keepdims=True)


def total(row):
    return jnp.sum(row, axis=1, keepdims=True)


def newton_direction(ga, gb, resid, direction, scal):
    d = resid + scal[2:3, :] * direction
    alpha = scal[0:1, :] / (total(ga + gb) + 0.05 * scal[1:2, :])
    return d, alpha


def start_kernel(count, rows, cols, parts, phi, band, out, scale, first, second, values):
    heavy = jax.nn.sigmoid(phi[...] / 0.5)
    scale[...] = band[...].astype(F32) * heavy * (1.0 - heavy) / 0.5
    forward_product(count, rows, cols, parts, heavy, out, first, second, values)
    aux_rows(out)


def restart_kernel(final, count, rows, cols, parts, phi, sa, sb, resid, direction, step, scal, *refs):
    if final:
        out, phi_out, first, second, values = refs
    else:
        band, out, phi_out, scale, first, second, values = refs
    d, alpha = newton_direction(sa[0:1, :], sb[0:1, :], resid[...], direction[...], scal[...])
    level = phi[...] + (step[...] + alpha * d)
    phi_out[...] = level
    heavy = jax.nn.sigmoid(level / 0.5)
    if not final:
        scale[...] = band[...].astype(F32) * heavy * (1.0 - heavy) / 0.5
    forward_product(count, rows, cols, parts, heavy, out, first, second, values)
    aux_rows(out)


def misfit_kernel(count, rows, cols, parts, q0, q1, q2, q3, observed, weight, out, first, second, values):
    q = q0[:128, :] + q1[:128, :] + q2[:128, :] + q3[:128, :]
    w = weight[...]
    adjoint_product(count, rows, cols, parts, w * w * (observed[...] - q), out, first, second, values)
    aux_rows(out)


def rhs_kernel(count, rows, cols, parts, ga, gb, scale, out, resid, first, second, values):
    rhs = scale[...] * (ga[:128, :] + gb[:128, :])
    resid[...] = rhs
    forward_product(count, rows, cols, parts, scale[...] * rhs, out, first, second, values)
    aux_rows(out, column_sum(rhs * rhs))


def push_values(q0, q1, q2, q3, weight, pushed, scal):
    t = q0[:128, :] + q1[:128, :] + q2[:128, :] + q3[:128, :]
    sums = q0[128:ROWS, :] + q1[128:ROWS, :] + q2[128:ROWS, :] + q3[128:ROWS, :]
    rr = total(sums[0:1, :]) + jnp.zeros((1, BS), F32)
    if pushed is None:
        beta, dd, q = jnp.zeros((1, BS), F32), rr, t
    else:
        rd = total(sums[1:2, :])
        beta = rr / scal[0:1, :]
        dd = rr + 2.0 * beta * rd + beta * beta * scal[1:2, :]
        q = t + beta * pushed[...]
    w = weight[...]
    u = w * w * q
    return rr, dd, beta, q, u


def store_scalars(scal_out, rr, dd, beta):
    scal_out[...] = jnp.zeros((8, BS), F32)
    scal_out[0:1, :] = rr
    scal_out[1:2, :] = dd
    scal_out[2:3, :] = beta


def push_kernel(first_turn, count, rows, cols, parts, q0, q1, q2, q3, weight, *refs):
    if first_turn:
        pushed = scal = None
    else:
        pushed, scal, *refs = refs
    out, q_out, scal_out, first, second, values = refs
    rr, dd, beta, q, u = push_values(q0, q1, q2, q3, weight, pushed, scal)
    q_out[...] = q
    store_scalars(scal_out, rr, dd, beta)
    adjoint_product(count, rows, cols, parts, u, out, first, second, values)
    aux_rows(out, column_sum(u * q))


def last_push_kernel(q0, q1, q2, q3, weight, pushed, scal, out, scal_out):
    rr, dd, beta, q, u = push_values(q0, q1, q2, q3, weight, pushed, scal)
    store_scalars(scal_out, rr, dd, beta)
    out[...] = jnp.zeros((8, BS), F32)
    out[0:1, :] = column_sum(u * q)


def turn_kernel(first_turn, count, rows, cols, parts, ga, gb, scale, band, scal, resid, *refs):
    if first_turn:
        out, resid_out, direction_out, step_out, first, second, values = refs
        direction, step = jnp.zeros((128, BS), F32), jnp.zeros((128, BS), F32)
    else:
        direction, step, out, resid_out, direction_out, step_out, first, second, values = refs
        direction, step = direction[...], step[...]
    d, alpha = newton_direction(ga[128:129, :], gb[128:129, :], resid[...], direction, scal[...])
    image = scale[...] * (ga[:128, :] + gb[:128, :]) + 0.05 * band[...].astype(F32) * d
    r = resid[...] - alpha * image
    direction_out[...] = d
    step_out[...] = step + alpha * d
    resid_out[...] = r
    forward_product(count, rows, cols, parts, scale[...] * r, out, first, second, values)
    aux_rows(out, column_sum(r * r), column_sum(r * d))


def per_device(
    sens_blocks, block_rows, block_cols, block_count, band_mask, level_set, observed, data_weight
):
    band = band_mask.reshape(128, BS)
    phi = level_set.reshape(128, BS)
    obs, weight = observed.reshape(128, BS), data_weight.reshape(128, BS)
    parts, flipped, *tables = split_blocks(
        block_count,
        block_rows.reshape(-1),
        block_cols.reshape(-1),
        sens_blocks.reshape(SLOTS, BS, BS),
    )
    tables = [pltpu.with_memory_space_constraint(t, pltpu.SMEM) for t in tables]
    wide, plain, small = (pltpu.VMEM((n, BS), F32) for n in (ROWS, 128, 8))

    def product(kernel, forward, operands, outs, name):
        return pl.pallas_call(
            kernel,
            out_shape=outs,
            in_specs=[SMEM] * 3 + [VMEM] * (1 + len(operands)),
            out_specs=[VMEM] * len(outs),
            scratch_shapes=TILES,
            compiler_params=PARAMS,
            name=name,
        )(*tables, flipped if forward else parts, *operands)

    def exchange(value, axis, size, partners):
        return [value] + [lax.ppermute(value, axis, [(i, i ^ p) for i in range(size)]) for p in partners]

    def over_col(value):
        z = exchange(value, "col", 16, (4, 12, 8))
        return exchange(z[0] + z[1] + z[2] + z[3], "col", 16, (1, 3, 2))

    def over_row(value):
        swap = [(i, i ^ 1) for i in range(8)]
        chip = value + lax.ppermute(value, "row", swap)
        far = lax.ppermute(chip, "row", [(i, i ^ 4) for i in range(8)])
        near = lax.ppermute(chip, "row", [(i, i ^ (6 if i % 2 else 2)) for i in range(8)])
        other = lax.ppermute(near, "row", swap)
        return chip + near + far, other

    update = None
    for outer in range(GN_ITERS):
        if update is None:
            out, scale = product(start_kernel, True, (phi, band), [wide, plain], "start")
        else:
            out, phi, scale = product(
                lambda *r: restart_kernel(False, *r), True, (*update, band), [wide, plain, plain], "restart"
            )
        (out,) = product(misfit_kernel, False, (*over_col(out), obs, weight), [wide], "misfit")
        out, resid = product(rhs_kernel, True, (*over_row(out), scale), [wide, plain], "rhs")
        state, pushed = (), ()
        for turn in range(CG_ITERS - 1):
            out, q, scal = product(
                lambda *r, one=turn == 0: push_kernel(one, *r),
                False,
                (*over_col(out), weight, *pushed),
                [wide, plain, small],
                "push",
            )
            pushed = (q, scal)
            out, resid, direction, step = product(
                lambda *r, one=turn == 0: turn_kernel(one, *r),
                True,
                (*over_row(out), scale, band, scal, resid, *state),
                [wide, plain, plain, plain],
                "turn",
            )
            state = (direction, step)
        sums, scal = pl.pallas_call(
            last_push_kernel,
            out_shape=[small, small],
            in_specs=[VMEM] * 7,
            out_specs=[VMEM] * 2,
            compiler_params=PARAMS,
            name="last_push",
        )(*over_col(out), weight, *pushed)
        update = (phi, *over_row(sums), resid, direction, step, scal)
    out, phi = product(lambda *r: restart_kernel(True, *r), True, update, [wide, plain], "final")
    q = over_col(out)
    misfit = weight * (obs - (q[0] + q[1] + q[2] + q[3])[:128])
    return phi.reshape(-1), misfit.reshape(-1)


def solution(mesh):
    return jax.shard_map(
        per_device,
        mesh=mesh,
        in_specs=(
            P("row", "col", None, None),
            P("row", "col"),
            P("row", "col"),
            P("row", "col"),
            P("col"),
            P("col"),
            P("row"),
            P("row"),
        ),
        out_specs=(P("col"), P("row")),
        check_vma=False,
    )
```

```python
import jax
import jax.numpy as jnp
from jax import lax
from jax.experimental import pallas as pl
from jax.experimental.pallas import tpu as pltpu
from jax.sharding import PartitionSpec as P

BS = 128
GN_ITERS = 2
CG_ITERS = 4
SLOTS = 192
GROUP = 48
CHUNK = 16
ROWS = 136
F32, BF16 = jnp.float32, jnp.bfloat16

VMEM = pl.BlockSpec(memory_space=pltpu.VMEM)
SMEM = pl.BlockSpec(memory_space=pltpu.SMEM)
PARAMS = pltpu.CompilerParams(vmem_limit_bytes=16 << 20)
TILES = [pltpu.VMEM((128, 16, 128), BF16), pltpu.VMEM((128, 16, 128), BF16), pltpu.VMEM((128, BS), F32)]


def groups(count):
    return (count[0] + GROUP - 1) // GROUP


def split_kernel(count_in, rows_in, cols_in, sens, parts, flipped, count, rows, cols, buf, sem, ids_sem):
    live = count_in[0, 0]
    chunks = (live + CHUNK - 1) // CHUNK
    count[0] = live
    row_copy = pltpu.make_async_copy(rows_in, rows, ids_sem.at[0])
    col_copy = pltpu.make_async_copy(cols_in, cols, ids_sem.at[1])
    row_copy.start()
    col_copy.start()

    def copy(g):
        at = pl.ds(g * CHUNK, CHUNK)
        return pltpu.make_async_copy(sens.at[at], buf.at[at], sem.at[g])

    def begin(g, carry):
        copy(g).start()
        return carry

    def body(g, carry):
        copy(g).wait()
        for b in range(CHUNK):
            k = g * CHUNK + b
            value = jnp.where(k < live, buf[k], 0.0)
            for to, v in ((parts, value), (flipped, value.T)):
                high = v.astype(BF16)
                to[k, :, :BS] = high
                to[k, :, BS:] = (v - high.astype(F32)).astype(BF16)
        return carry

    def clear(g, carry):
        at = pl.ds(g * CHUNK, CHUNK)
        parts[at] = jnp.zeros((CHUNK, BS, 2 * BS), BF16)
        flipped[at] = jnp.zeros((CHUNK, BS, 2 * BS), BF16)
        return carry

    lax.fori_loop(0, chunks, begin, 0)
    lax.fori_loop(chunks, groups(count) * (GROUP // CHUNK), clear, 0)
    lax.fori_loop(0, chunks, body, 0)
    row_copy.wait()
    col_copy.wait()


def split_blocks(count, rows, cols, sens):
    halves = pltpu.VMEM((SLOTS, BS, 2 * BS), BF16)
    hbm = pl.BlockSpec(memory_space=pltpu.HBM)
    return pl.pallas_call(
        split_kernel,
        out_shape=[halves, halves]
        + [pltpu.SMEM((n,), jnp.int32) for n in (1, SLOTS, SLOTS)],
        in_specs=[SMEM, hbm, hbm, hbm],
        out_specs=[VMEM, VMEM, SMEM, SMEM, SMEM],
        scratch_shapes=[
            pltpu.VMEM((SLOTS, BS, BS), F32),
            pltpu.SemaphoreType.DMA((SLOTS // CHUNK,)),
            pltpu.SemaphoreType.DMA((2,)),
        ],
        compiler_params=PARAMS,
        name="split_blocks",
    )(count, *(pltpu.with_memory_space_constraint(v, pltpu.HBM) for v in (rows, cols, sens)))


def fill_tiles(x, first, second):
    high = x.astype(BF16).astype(F32)
    low = x - high
    at = lax.broadcasted_iota(jnp.int32, (128, 8, BS), 1)
    high, low = high[:, None, :], low[:, None, :]
    for to, row in ((first, 0), (second, 2)):
        tile = jnp.where(at == row, high, jnp.where(at == row + 1, low, 0.0))
        to[...] = jnp.concatenate([tile, tile], axis=1).astype(BF16)


def product_of(count, source, target, parts, x, out, first, second, values):
    fill_tiles(x, first, second)
    values[...] = x
    out[...] = jnp.zeros_like(out)

    def matrix_pair(k):
        r = lax.dot_general(
            jnp.concatenate([first[source[k]], second[source[k + 1]]], axis=1),
            parts[pl.ds(k, 2)].reshape(2 * BS, 2 * BS),
            (((1,), (0,)), ((), ())),
            preferred_element_type=F32,
        )
        r = r[0:8, :BS] + r[0:8, BS:]
        out[pl.ds(target[k], 1), :] += r[0:1] + r[1:2]
        out[pl.ds(target[k + 1], 1), :] += r[2:3] + r[3:4]

    def vector_block(k):
        weights = jnp.broadcast_to(values[pl.ds(source[k], 1), :], (BS, BS)).T
        block = parts[k]
        terms = (block[:, :BS].astype(F32) + block[:, BS:].astype(F32)) * weights
        terms = jnp.sum(terms.reshape(BS // 8, 8, BS), axis=0)
        out[pl.ds(target[k], 1), :] += jnp.sum(terms, axis=0, keepdims=True)

    def body(g, carry):
        for at in range(0, GROUP, 16):
            k = g * GROUP + at
            for p in range(0, 10, 2):
                matrix_pair(k + p)
            for p in range(10, 16):
                vector_block(k + p)
        return carry

    lax.fori_loop(0, groups(count), body, 0)


def forward_product(count, rows, cols, flipped, x, out, first, second, values):
    product_of(count, cols, rows, flipped, x, out, first, second, values)


def adjoint_product(count, rows, cols, parts, x, out, first, second, values):
    product_of(count, rows, cols, parts, x, out, first, second, values)


def aux_rows(out, *vectors):
    out[128:ROWS, :] = jnp.zeros((8, BS), F32)
    for i, v in enumerate(vectors):
        out[128 + i : 129 + i, :] = v


def column_sum(x):
    return jnp.sum(x, axis=0, keepdims=True)


def total(row):
    return jnp.sum(row, axis=1, keepdims=True)


def newton_direction(ga, gb, resid, direction, scal):
    d = resid + scal[2:3, :] * direction
    alpha = scal[0:1, :] / (total(ga + gb) + 0.05 * scal[1:2, :])
    return d, alpha


def start_kernel(count, rows, cols, parts, phi, band, out, scale, first, second, values):
    heavy = jax.nn.sigmoid(phi[...] / 0.5)
    scale[...] = band[...].astype(F32) * heavy * (1.0 - heavy) / 0.5
    forward_product(count, rows, cols, parts, heavy, out, first, second, values)
    aux_rows(out)


def restart_kernel(final, count, rows, cols, parts, phi, sa, sb, resid, direction, step, scal, *refs):
    if final:
        out, phi_out, first, second, values = refs
    else:
        band, out, phi_out, scale, first, second, values = refs
    d, alpha = newton_direction(sa[0:1, :], sb[0:1, :], resid[...], direction[...], scal[...])
    level = phi[...] + (step[...] + alpha * d)
    phi_out[...] = level
    heavy = jax.nn.sigmoid(level / 0.5)
    if not final:
        scale[...] = band[...].astype(F32) * heavy * (1.0 - heavy) / 0.5
    forward_product(count, rows, cols, parts, heavy, out, first, second, values)
    aux_rows(out)


def misfit_kernel(count, rows, cols, parts, q0, q1, q2, q3, observed, weight, out, first, second, values):
    q = q0[:128, :] + q1[:128, :] + q2[:128, :] + q3[:128, :]
    w = weight[...]
    adjoint_product(count, rows, cols, parts, w * w * (observed[...] - q), out, first, second, values)
    aux_rows(out)


def rhs_kernel(count, rows, cols, parts, ga, gb, scale, out, resid, first, second, values):
    rhs = scale[...] * (ga[:128, :] + gb[:128, :])
    resid[...] = rhs
    forward_product(count, rows, cols, parts, scale[...] * rhs, out, first, second, values)
    aux_rows(out, column_sum(rhs * rhs))


def push_values(q0, q1, q2, q3, weight, pushed, scal):
    t = q0[:128, :] + q1[:128, :] + q2[:128, :] + q3[:128, :]
    sums = q0[128:ROWS, :] + q1[128:ROWS, :] + q2[128:ROWS, :] + q3[128:ROWS, :]
    rr = total(sums[0:1, :]) + jnp.zeros((1, BS), F32)
    if pushed is None:
        beta, dd, q = jnp.zeros((1, BS), F32), rr, t
    else:
        rd = total(sums[1:2, :])
        beta = rr / scal[0:1, :]
        dd = rr + 2.0 * beta * rd + beta * beta * scal[1:2, :]
        q = t + beta * pushed[...]
    w = weight[...]
    u = w * w * q
    return rr, dd, beta, q, u


def store_scalars(scal_out, rr, dd, beta):
    scal_out[...] = jnp.zeros((8, BS), F32)
    scal_out[0:1, :] = rr
    scal_out[1:2, :] = dd
    scal_out[2:3, :] = beta


def push_kernel(first_turn, count, rows, cols, parts, q0, q1, q2, q3, weight, *refs):
    if first_turn:
        pushed = scal = None
    else:
        pushed, scal, *refs = refs
    out, q_out, scal_out, first, second, values = refs
    rr, dd, beta, q, u = push_values(q0, q1, q2, q3, weight, pushed, scal)
    q_out[...] = q
    store_scalars(scal_out, rr, dd, beta)
    adjoint_product(count, rows, cols, parts, u, out, first, second, values)
    aux_rows(out, column_sum(u * q))


def last_push_kernel(q0, q1, q2, q3, weight, pushed, scal, out, scal_out):
    rr, dd, beta, q, u = push_values(q0, q1, q2, q3, weight, pushed, scal)
    store_scalars(scal_out, rr, dd, beta)
    out[...] = jnp.zeros((8, BS), F32)
    out[0:1, :] = column_sum(u * q)


def turn_kernel(first_turn, count, rows, cols, parts, ga, gb, scale, band, scal, resid, *refs):
    if first_turn:
        out, resid_out, direction_out, step_out, first, second, values = refs
        direction, step = jnp.zeros((128, BS), F32), jnp.zeros((128, BS), F32)
    else:
        direction, step, out, resid_out, direction_out, step_out, first, second, values = refs
        direction, step = direction[...], step[...]
    d, alpha = newton_direction(ga[128:129, :], gb[128:129, :], resid[...], direction, scal[...])
    image = scale[...] * (ga[:128, :] + gb[:128, :]) + 0.05 * band[...].astype(F32) * d
    r = resid[...] - alpha * image
    direction_out[...] = d
    step_out[...] = step + alpha * d
    resid_out[...] = r
    forward_product(count, rows, cols, parts, scale[...] * r, out, first, second, values)
    aux_rows(out, column_sum(r * r), column_sum(r * d))


def per_device(
    sens_blocks, block_rows, block_cols, block_count, band_mask, level_set, observed, data_weight
):
    band = band_mask.reshape(128, BS)
    phi = level_set.reshape(128, BS)
    obs, weight = observed.reshape(128, BS), data_weight.reshape(128, BS)
    parts, flipped, *tables = split_blocks(
        block_count,
        block_rows.reshape(-1),
        block_cols.reshape(-1),
        sens_blocks.reshape(SLOTS, BS, BS),
    )
    tables = [pltpu.with_memory_space_constraint(t, pltpu.SMEM) for t in tables]
    wide, plain, small = (pltpu.VMEM((n, BS), F32) for n in (ROWS, 128, 8))

    def product(kernel, forward, operands, outs, name):
        return pl.pallas_call(
            kernel,
            out_shape=outs,
            in_specs=[SMEM] * 3 + [VMEM] * (1 + len(operands)),
            out_specs=[VMEM] * len(outs),
            scratch_shapes=TILES,
            compiler_params=PARAMS,
            name=name,
        )(*tables, flipped if forward else parts, *operands)

    def exchange(value, axis, size, partners):
        return [value] + [lax.ppermute(value, axis, [(i, i ^ p) for i in range(size)]) for p in partners]

    def over_col(value):
        z = exchange(value, "col", 16, (4, 12, 8))
        return exchange(z[0] + z[1] + z[2] + z[3], "col", 16, (1, 3, 2))

    def over_row(value):
        swap = [(i, i ^ 1) for i in range(8)]
        chip = value + lax.ppermute(value, "row", swap)
        far = lax.ppermute(chip, "row", [(i, i ^ 4) for i in range(8)])
        near = lax.ppermute(chip, "row", [(i, i ^ (6 if i % 2 else 2)) for i in range(8)])
        other = lax.ppermute(near, "row", swap)
        return chip + near + far, other

    update = None
    for outer in range(GN_ITERS):
        if update is None:
            out, scale = product(start_kernel, True, (phi, band), [wide, plain], "start")
        else:
            out, phi, scale = product(
                lambda *r: restart_kernel(False, *r), True, (*update, band), [wide, plain, plain], "restart"
            )
        (out,) = product(misfit_kernel, False, (*over_col(out), obs, weight), [wide], "misfit")
        out, resid = product(rhs_kernel, True, (*over_row(out), scale), [wide, plain], "rhs")
        state, pushed = (), ()
        for turn in range(CG_ITERS - 1):
            out, q, scal = product(
                lambda *r, one=turn == 0: push_kernel(one, *r),
                False,
                (*over_col(out), weight, *pushed),
                [wide, plain, small],
                "push",
            )
            pushed = (q, scal)
            out, resid, direction, step = product(
                lambda *r, one=turn == 0: turn_kernel(one, *r),
                True,
                (*over_row(out), scale, band, scal, resid, *state),
                [wide, plain, plain, plain],
                "turn",
            )
            state = (direction, step)
        sums, scal = pl.pallas_call(
            last_push_kernel,
            out_shape=[small, small],
            in_specs=[VMEM] * 7,
            out_specs=[VMEM] * 2,
            compiler_params=PARAMS,
            name="last_push",
        )(*over_col(out), weight, *pushed)
        update = (phi, *over_row(sums), resid, direction, step, scal)
    out, phi = product(lambda *r: restart_kernel(True, *r), True, update, [wide, plain], "final")
    q = over_col(out)
    misfit = weight * (obs - (q[0] + q[1] + q[2] + q[3])[:128])
    return phi.reshape(-1), misfit.reshape(-1)


def solution(mesh):
    return jax.shard_map(
        per_device,
        mesh=mesh,
        in_specs=(
            P("row", "col", None, None),
            P("row", "col"),
            P("row", "col"),
            P("row", "col"),
            P("col"),
            P("col"),
            P("row"),
            P("row"),
        ),
        out_specs=(P("col"), P("row")),
        check_vma=False,
    )
```

```python
import jax
import jax.numpy as jnp
from jax import lax
from jax.experimental import pallas as pl
from jax.experimental.pallas import tpu as pltpu
from jax.sharding import PartitionSpec as P

BS = 128
GN_ITERS = 2
CG_ITERS = 4
SLOTS = 192
GROUP = 48
CHUNK = 16
ROWS = 136
F32, BF16 = jnp.float32, jnp.bfloat16

VMEM = pl.BlockSpec(memory_space=pltpu.VMEM)
SMEM = pl.BlockSpec(memory_space=pltpu.SMEM)
PARAMS = pltpu.CompilerParams(vmem_limit_bytes=16 << 20)
TILES = [pltpu.VMEM((128, 16, 128), BF16), pltpu.VMEM((128, 16, 128), BF16), pltpu.VMEM((128, BS), F32)]


def groups(count):
    return (count[0] + GROUP - 1) // GROUP


def split_kernel(count_in, rows_in, cols_in, sens, parts, flipped, count, rows, cols, buf, sem, ids_sem):
    live = count_in[0, 0]
    chunks = (live + CHUNK - 1) // CHUNK
    count[0] = live
    row_copy = pltpu.make_async_copy(rows_in, rows, ids_sem.at[0])
    col_copy = pltpu.make_async_copy(cols_in, cols, ids_sem.at[1])
    row_copy.start()
    col_copy.start()

    def copy(g):
        at = pl.ds(g * CHUNK, CHUNK)
        return pltpu.make_async_copy(sens.at[at], buf.at[at], sem.at[g])

    def begin(g, carry):
        copy(g).start()
        return carry

    def body(g, carry):
        copy(g).wait()
        for b in range(CHUNK):
            k = g * CHUNK + b
            value = jnp.where(k < live, buf[k], 0.0)
            for to, v in ((parts, value), (flipped, value.T)):
                high = v.astype(BF16)
                to[k, :, :BS] = high
                to[k, :, BS:] = (v - high.astype(F32)).astype(BF16)
        return carry

    def clear(g, carry):
        at = pl.ds(g * CHUNK, CHUNK)
        parts[at] = jnp.zeros((CHUNK, BS, 2 * BS), BF16)
        flipped[at] = jnp.zeros((CHUNK, BS, 2 * BS), BF16)
        return carry

    lax.fori_loop(0, chunks, begin, 0)
    lax.fori_loop(chunks, groups(count) * (GROUP // CHUNK), clear, 0)
    lax.fori_loop(0, chunks, body, 0)
    row_copy.wait()
    col_copy.wait()


def split_blocks(count, rows, cols, sens):
    halves = pltpu.VMEM((SLOTS, BS, 2 * BS), BF16)
    hbm = pl.BlockSpec(memory_space=pltpu.HBM)
    return pl.pallas_call(
        split_kernel,
        out_shape=[halves, halves]
        + [pltpu.SMEM((n,), jnp.int32) for n in (1, SLOTS, SLOTS)],
        in_specs=[SMEM, hbm, hbm, hbm],
        out_specs=[VMEM, VMEM, SMEM, SMEM, SMEM],
        scratch_shapes=[
            pltpu.VMEM((SLOTS, BS, BS), F32),
            pltpu.SemaphoreType.DMA((SLOTS // CHUNK,)),
            pltpu.SemaphoreType.DMA((2,)),
        ],
        compiler_params=PARAMS,
        name="split_blocks",
    )(count, *(pltpu.with_memory_space_constraint(v, pltpu.HBM) for v in (rows, cols, sens)))


def fill_tiles(x, first, second):
    high = x.astype(BF16).astype(F32)
    low = x - high
    at = lax.broadcasted_iota(jnp.int32, (128, 8, BS), 1)
    high, low = high[:, None, :], low[:, None, :]
    for to, row in ((first, 0), (second, 2)):
        tile = jnp.where(at == row, high, jnp.where(at == row + 1, low, 0.0))
        to[...] = jnp.concatenate([tile, tile], axis=1).astype(BF16)


def product_of(count, source, target, parts, x, out, first, second, values):
    fill_tiles(x, first, second)
    values[...] = x
    out[...] = jnp.zeros_like(out)

    def matrix_pair(k):
        r = lax.dot_general(
            jnp.concatenate([first[source[k]], second[source[k + 1]]], axis=1),
            parts[pl.ds(k, 2)].reshape(2 * BS, 2 * BS),
            (((1,), (0,)), ((), ())),
            preferred_element_type=F32,
        )
        r = r[0:8, :BS] + r[0:8, BS:]
        out[pl.ds(target[k], 1), :] += r[0:1] + r[1:2]
        out[pl.ds(target[k + 1], 1), :] += r[2:3] + r[3:4]

    def vector_block(k):
        weights = jnp.broadcast_to(values[pl.ds(source[k], 1), :], (BS, BS)).T
        block = parts[k]
        terms = (block[:, :BS].astype(F32) + block[:, BS:].astype(F32)) * weights
        terms = jnp.sum(terms.reshape(BS // 8, 8, BS), axis=0)
        out[pl.ds(target[k], 1), :] += jnp.sum(terms, axis=0, keepdims=True)

    def body(g, carry):
        for at in range(0, GROUP, 16):
            k = g * GROUP + at
            for p in range(5):
                matrix_pair(k + 2 * p)
                vector_block(k + 10 + p)
            vector_block(k + 15)
        return carry

    lax.fori_loop(0, groups(count), body, 0)


def forward_product(count, rows, cols, flipped, x, out, first, second, values):
    product_of(count, cols, rows, flipped, x, out, first, second, values)


def adjoint_product(count, rows, cols, parts, x, out, first, second, values):
    product_of(count, rows, cols, parts, x, out, first, second, values)


def aux_rows(out, *vectors):
    out[128:ROWS, :] = jnp.zeros((8, BS), F32)
    for i, v in enumerate(vectors):
        out[128 + i : 129 + i, :] = v


def column_sum(x):
    return jnp.sum(x, axis=0, keepdims=True)


def total(row):
    return jnp.sum(row, axis=1, keepdims=True)


def newton_direction(ga, gb, resid, direction, scal):
    d = resid + scal[2:3, :] * direction
    alpha = scal[0:1, :] / (total(ga + gb) + 0.05 * scal[1:2, :])
    return d, alpha


def start_kernel(count, rows, cols, parts, phi, band, out, scale, first, second, values):
    heavy = jax.nn.sigmoid(phi[...] / 0.5)
    scale[...] = band[...].astype(F32) * heavy * (1.0 - heavy) / 0.5
    forward_product(count, rows, cols, parts, heavy, out, first, second, values)
    aux_rows(out)


def restart_kernel(final, count, rows, cols, parts, phi, sa, sb, resid, direction, step, scal, *refs):
    if final:
        out, phi_out, first, second, values = refs
    else:
        band, out, phi_out, scale, first, second, values = refs
    d, alpha = newton_direction(sa[0:1, :], sb[0:1, :], resid[...], direction[...], scal[...])
    level = phi[...] + (step[...] + alpha * d)
    phi_out[...] = level
    heavy = jax.nn.sigmoid(level / 0.5)
    if not final:
        scale[...] = band[...].astype(F32) * heavy * (1.0 - heavy) / 0.5
    forward_product(count, rows, cols, parts, heavy, out, first, second, values)
    aux_rows(out)


def misfit_kernel(count, rows, cols, parts, q0, q1, q2, q3, observed, weight, out, first, second, values):
    q = q0[:128, :] + q1[:128, :] + q2[:128, :] + q3[:128, :]
    w = weight[...]
    adjoint_product(count, rows, cols, parts, w * w * (observed[...] - q), out, first, second, values)
    aux_rows(out)


def rhs_kernel(count, rows, cols, parts, ga, gb, scale, out, resid, first, second, values):
    rhs = scale[...] * (ga[:128, :] + gb[:128, :])
    resid[...] = rhs
    forward_product(count, rows, cols, parts, scale[...] * rhs, out, first, second, values)
    aux_rows(out, column_sum(rhs * rhs))


def push_values(q0, q1, q2, q3, weight, pushed, scal):
    t = q0[:128, :] + q1[:128, :] + q2[:128, :] + q3[:128, :]
    sums = q0[128:ROWS, :] + q1[128:ROWS, :] + q2[128:ROWS, :] + q3[128:ROWS, :]
    rr = total(sums[0:1, :]) + jnp.zeros((1, BS), F32)
    if pushed is None:
        beta, dd, q = jnp.zeros((1, BS), F32), rr, t
    else:
        rd = total(sums[1:2, :])
        beta = rr / scal[0:1, :]
        dd = rr + 2.0 * beta * rd + beta * beta * scal[1:2, :]
        q = t + beta * pushed[...]
    w = weight[...]
    u = w * w * q
    return rr, dd, beta, q, u


def store_scalars(scal_out, rr, dd, beta):
    scal_out[...] = jnp.zeros((8, BS), F32)
    scal_out[0:1, :] = rr
    scal_out[1:2, :] = dd
    scal_out[2:3, :] = beta


def push_kernel(first_turn, count, rows, cols, parts, q0, q1, q2, q3, weight, *refs):
    if first_turn:
        pushed = scal = None
    else:
        pushed, scal, *refs = refs
    out, q_out, scal_out, first, second, values = refs
    rr, dd, beta, q, u = push_values(q0, q1, q2, q3, weight, pushed, scal)
    q_out[...] = q
    store_scalars(scal_out, rr, dd, beta)
    adjoint_product(count, rows, cols, parts, u, out, first, second, values)
    aux_rows(out, column_sum(u * q))


def last_push_kernel(q0, q1, q2, q3, weight, pushed, scal, out, scal_out):
    rr, dd, beta, q, u = push_values(q0, q1, q2, q3, weight, pushed, scal)
    store_scalars(scal_out, rr, dd, beta)
    out[...] = jnp.zeros((8, BS), F32)
    out[0:1, :] = column_sum(u * q)


def turn_kernel(first_turn, count, rows, cols, parts, ga, gb, scale, band, scal, resid, *refs):
    if first_turn:
        out, resid_out, direction_out, step_out, first, second, values = refs
        direction, step = jnp.zeros((128, BS), F32), jnp.zeros((128, BS), F32)
    else:
        direction, step, out, resid_out, direction_out, step_out, first, second, values = refs
        direction, step = direction[...], step[...]
    d, alpha = newton_direction(ga[128:129, :], gb[128:129, :], resid[...], direction, scal[...])
    image = scale[...] * (ga[:128, :] + gb[:128, :]) + 0.05 * band[...].astype(F32) * d
    r = resid[...] - alpha * image
    direction_out[...] = d
    step_out[...] = step + alpha * d
    resid_out[...] = r
    forward_product(count, rows, cols, parts, scale[...] * r, out, first, second, values)
    aux_rows(out, column_sum(r * r), column_sum(r * d))


def per_device(
    sens_blocks, block_rows, block_cols, block_count, band_mask, level_set, observed, data_weight
):
    band = band_mask.reshape(128, BS)
    phi = level_set.reshape(128, BS)
    obs, weight = observed.reshape(128, BS), data_weight.reshape(128, BS)
    parts, flipped, *tables = split_blocks(
        block_count,
        block_rows.reshape(-1),
        block_cols.reshape(-1),
        sens_blocks.reshape(SLOTS, BS, BS),
    )
    tables = [pltpu.with_memory_space_constraint(t, pltpu.SMEM) for t in tables]
    wide, plain, small = (pltpu.VMEM((n, BS), F32) for n in (ROWS, 128, 8))

    def product(kernel, forward, operands, outs, name):
        return pl.pallas_call(
            kernel,
            out_shape=outs,
            in_specs=[SMEM] * 3 + [VMEM] * (1 + len(operands)),
            out_specs=[VMEM] * len(outs),
            scratch_shapes=TILES,
            compiler_params=PARAMS,
            name=name,
        )(*tables, flipped if forward else parts, *operands)

    def exchange(value, axis, size, partners):
        return [value] + [lax.ppermute(value, axis, [(i, i ^ p) for i in range(size)]) for p in partners]

    def over_col(value):
        z = exchange(value, "col", 16, (4, 12, 8))
        return exchange(z[0] + z[1] + z[2] + z[3], "col", 16, (1, 3, 2))

    def over_row(value):
        swap = [(i, i ^ 1) for i in range(8)]
        chip = value + lax.ppermute(value, "row", swap)
        far = lax.ppermute(chip, "row", [(i, i ^ 4) for i in range(8)])
        near = lax.ppermute(chip, "row", [(i, i ^ (6 if i % 2 else 2)) for i in range(8)])
        other = lax.ppermute(near, "row", swap)
        return chip + near + far, other

    update = None
    for outer in range(GN_ITERS):
        if update is None:
            out, scale = product(start_kernel, True, (phi, band), [wide, plain], "start")
        else:
            out, phi, scale = product(
                lambda *r: restart_kernel(False, *r), True, (*update, band), [wide, plain, plain], "restart"
            )
        (out,) = product(misfit_kernel, False, (*over_col(out), obs, weight), [wide], "misfit")
        out, resid = product(rhs_kernel, True, (*over_row(out), scale), [wide, plain], "rhs")
        state, pushed = (), ()
        for turn in range(CG_ITERS - 1):
            out, q, scal = product(
                lambda *r, one=turn == 0: push_kernel(one, *r),
                False,
                (*over_col(out), weight, *pushed),
                [wide, plain, small],
                "push",
            )
            pushed = (q, scal)
            out, resid, direction, step = product(
                lambda *r, one=turn == 0: turn_kernel(one, *r),
                True,
                (*over_row(out), scale, band, scal, resid, *state),
                [wide, plain, plain, plain],
                "turn",
            )
            state = (direction, step)
        sums, scal = pl.pallas_call(
            last_push_kernel,
            out_shape=[small, small],
            in_specs=[VMEM] * 7,
            out_specs=[VMEM] * 2,
            compiler_params=PARAMS,
            name="last_push",
        )(*over_col(out), weight, *pushed)
        update = (phi, *over_row(sums), resid, direction, step, scal)
    out, phi = product(lambda *r: restart_kernel(True, *r), True, update, [wide, plain], "final")
    q = over_col(out)
    misfit = weight * (obs - (q[0] + q[1] + q[2] + q[3])[:128])
    return phi.reshape(-1), misfit.reshape(-1)


def solution(mesh):
    return jax.shard_map(
        per_device,
        mesh=mesh,
        in_specs=(
            P("row", "col", None, None),
            P("row", "col"),
            P("row", "col"),
            P("row", "col"),
            P("col"),
            P("col"),
            P("row"),
            P("row"),
        ),
        out_specs=(P("col"), P("row")),
        check_vma=False,
    )
```
